512 devices in a mesh: section: 64 (over y, z_lo, core), coil: 8 (over z_hi, x).
Axes of the slice: x: 4, y: 4, z: 16 (z_hi: 2, z_lo: 8; z = z_hi * 8 + z_lo), core: 2. Of those that a mesh axis runs over, the one named last changes fastest.
Arguments:
- kspace: bfloat16 [16, 64, 64, 640], P('coil', None, 'section'), may hold values from -6 to 6
- coil_maps: bfloat16 [16, 64, 64, 640], P('coil', 'section'), may hold values from -1.5 to 1.5
- sampling: int32 [2, 32, 320], replicated, may hold values 0 or 1
- dc_weight: float32 [2], replicated, may hold values from 0.5 to 2.5
- kernel_in: float32 [2, 9, 18, 2], replicated, may hold values from -1.5 to 1.5
- bias_in: float32 [2, 18], replicated, may hold values from -0.5 to 0.5
- kernel_out: float32 [2, 9, 2, 18], replicated, may hold values from -0.5 to 0.5
- bias_out: float32 [2, 2], replicated, may hold values from -0.5 to 0.5
- cotangent: bfloat16 [64, 64, 640], P('section'), may hold values from -6 to 6
Outputs:
- image_out: float32 [64, 64, 640], P('section')
- grad_kspace: float32 [16, 64, 64, 640], P('coil', None, 'section')
The draws below stay inside these ranges and needn't reach their ends.
All inputs are finite; a program needn't handle non-finite values.
Results may differ from the reference program's by a relative error of at most 0.035.
Values may be sent and summed in bfloat16 or wider, within the bound.
A program may use at most 64 MiB of HBM per device.

```python
import math
import jax
import jax.numpy as jnp
from jax import lax

COILS = 16
LINES = 320
CHANNELS = 18
CASCADES = 2
VOLUMES = 2
ROWS = 64
SLOTS = 64
DEPTH = 32


def plant(drawn, stream_key, low, high):
    longest = drawn.shape.index(max(drawn.shape))
    spots = []
    for shift in (0, 1):
        where = [jax.random.randint(jax.random.fold_in(stream_key, axis), (), 0, length) for axis, length in enumerate(drawn.shape)]
        where[longest] = (where[longest] + shift) % drawn.shape[longest]
        spots.append(tuple(where))
    return drawn.at[spots[0]].set(low).at[spots[1]].set(high)


def block_levels(own_key, dims, shards, least, high):
    loudness = 1.0
    for axis_at, parts in shards:
        steps = jax.random.uniform(jax.random.fold_in(jax.random.fold_in(own_key, 6), axis_at), (parts,), jnp.float32, least / len(shards), high / len(shards))
        loudness = loudness * jnp.repeat(jnp.exp(steps), dims[axis_at] // parts).reshape((-1,) + (1,) * (len(dims) - 1 - axis_at))
    return loudness


def normal_values(key, shape, width, reach, split=(), kind=jnp.bfloat16):
    level = block_levels(key, shape, split, -0.22, 0.18) if split else 1.0
    entries = jax.random.normal(key, shape, jnp.float32) * width * level
    return jnp.minimum(jnp.maximum(entries, -reach), reach).astype(kind)


def setup_inputs(seed: int = 0) -> dict:
    splits = jax.random.split(jax.random.key(seed), 10)
    return {
        "kspace": normal_values(splits[0], (COILS, SLOTS, ROWS, 2 * LINES), 1.0, 6.0, ((0, 8), (2, 64))),
        "coil_maps": normal_values(splits[1], (COILS, SLOTS, ROWS, 2 * LINES), COILS ** -0.5, 1.5, ((0, 8), (1, 64))),
        "sampling": plant((jax.random.randint(splits[2], (VOLUMES, DEPTH, LINES), 0, 3) < 1).astype(jnp.int32), jax.random.fold_in(splits[2], 1), 0, 1),
        "dc_weight": jnp.clip(jax.random.uniform(splits[3], (CASCADES,), jnp.float32, 0.5, 2.5), 0.5, 2.5),
        "kernel_in": normal_values(splits[4], (CASCADES, 9, CHANNELS, 2), 18 ** -0.5, 1.5, (), jnp.float32),
        "bias_in": jnp.clip(jax.random.uniform(splits[5], (CASCADES, CHANNELS), jnp.float32, -0.5, 0.5), -0.5, 0.5),
        "kernel_out": normal_values(splits[6], (CASCADES, 9, 2, CHANNELS), (9 * CHANNELS) ** -0.5, 0.5, (), jnp.float32),
        "bias_out": jnp.clip(jax.random.uniform(splits[7], (CASCADES, 2), jnp.float32, -0.5, 0.5), -0.5, 0.5),
        "cotangent": normal_values(splits[8], (SLOTS, ROWS, 2 * LINES), 1.0, 6.0, ((0, 64),)),
    }


PRECISE = lax.Precision.HIGHEST

def line_table(count, exponent_sign):
    indices = jnp.arange(count, dtype=jnp.int32)
    product = indices[:, None] * indices[None, :] % count
    angles = product.astype(jnp.float32) * (2.0 * math.pi / count)
    factor = 1.0 / math.sqrt(count)
    return (jnp.cos(angles) * factor, exponent_sign * jnp.sin(angles) * factor)

def to_bf(values):
    return lax.optimization_barrier(values.astype(jnp.bfloat16)).astype(jnp.float32)

def line_matrix(count, exponent_sign):
    real_part, imag_part = line_table(count, exponent_sign)
    upper_rows = jnp.concatenate([real_part, imag_part], axis=1)
    lower_rows = jnp.concatenate([-imag_part, real_part], axis=1)
    return to_bf(jnp.concatenate([upper_rows, lower_rows], axis=0))

def line_transform(values, matrix):
    return jnp.dot(to_bf(values), matrix, precision=PRECISE, preferred_element_type=jnp.float32)

def depth_transform(values, volumes, exponent_sign):
    layout_shape = values.shape
    width_two = layout_shape[-1]
    half_width = width_two // 2
    depth_count = layout_shape[1] // volumes
    real_part, imag_part = line_table(depth_count, exponent_sign)
    blocks = to_bf(values).reshape(layout_shape[0], volumes, depth_count, layout_shape[2], width_two)
    straight = jnp.einsum('kz,cvzrw->cvkrw', to_bf(real_part), blocks, precision=PRECISE)
    crossed = jnp.einsum('kz,cvzrw->cvkrw', to_bf(imag_part), blocks, precision=PRECISE)
    turned = jnp.concatenate([-crossed[..., half_width:], crossed[..., :half_width]], axis=-1)
    return (straight + turned).reshape(layout_shape)

def spread(coil_maps, picture):
    half_width = coil_maps.shape[-1] // 2
    maps_real = coil_maps[..., :half_width].astype(jnp.float32)
    maps_imag = coil_maps[..., half_width:].astype(jnp.float32)
    pic_real = picture[..., :half_width].astype(jnp.float32)
    pic_imag = picture[..., half_width:].astype(jnp.float32)
    return jnp.concatenate([maps_real * pic_real - maps_imag * pic_imag, maps_real * pic_imag + maps_imag * pic_real], axis=-1)

def collect(coil_maps, coil_images):
    half_width = coil_maps.shape[-1] // 2
    maps_real = coil_maps[..., :half_width].astype(jnp.float32)
    maps_imag = coil_maps[..., half_width:].astype(jnp.float32)
    img_real = coil_images[..., :half_width]
    img_imag = coil_images[..., half_width:]
    summed = jnp.concatenate([maps_real * img_real + maps_imag * img_imag, maps_real * img_imag - maps_imag * img_real], axis=-1)
    return lax.optimization_barrier(jnp.sum(summed, axis=0))

def shifted_windows(planes):
    row_count, col_count = (planes.shape[-2], planes.shape[-1])
    padded = jnp.pad(planes, ((0, 0), (1, 1), (1, 1)))
    return jnp.stack([padded[:, row_shift:row_shift + row_count, col_shift:col_shift + col_count] for row_shift in range(3) for col_shift in range(3)], axis=0)

def conv_out(hidden, kernel, bias):
    row_count, col_count = (hidden.shape[-2], hidden.shape[-1])
    projected = jnp.einsum('toc,cxy->toxy', kernel, hidden, precision=PRECISE)
    padded = jnp.pad(projected, ((0, 0), (0, 0), (1, 1), (1, 1)))
    summed = jnp.zeros((kernel.shape[1], row_count, col_count), jnp.float32) + bias[:, None, None]
    for tap_index in range(9):
        row_shift = tap_index // 3
        col_shift = tap_index % 3
        summed = summed + padded[tap_index, :, row_shift:row_shift + row_count, col_shift:col_shift + col_count]
    return summed

def refine(picture, kernel_in, bias_in, kernel_out, bias_out):
    half_width = picture.shape[-1] // 2
    planes = jnp.stack([picture[:, :half_width], picture[:, half_width:]], axis=0)
    hidden = jnp.einsum('toc,tcxy->oxy', kernel_in, shifted_windows(planes), precision=PRECISE) + bias_in[:, None, None]
    hidden = jax.nn.silu(hidden)
    output = conv_out(hidden, kernel_out, bias_out)
    return jnp.concatenate([output[0], output[1]], axis=1)

def reference(kspace, coil_maps, sampling, dc_weight, kernel_in, bias_in, kernel_out, bias_out, cotangent):
    lines_used = sampling.astype(jnp.float32).reshape(SLOTS, LINES)
    sampled = jnp.concatenate([lines_used, lines_used], axis=1)[None, :, None, :]
    measured = sampled * kspace.astype(jnp.float32)
    forward_line = line_matrix(LINES, -1.0)
    inverse_line = line_matrix(LINES, 1.0)

    def expand(picture):
        return depth_transform(line_transform(spread(coil_maps, picture[None]), forward_line), VOLUMES, -1.0)

    def combine(kstate):
        return collect(coil_maps, line_transform(depth_transform(kstate, VOLUMES, 1.0), inverse_line))
    refine_all = jax.vmap(refine, in_axes=(0, None, None, None, None))
    kstate = measured
    stored = []
    for cascade in range(CASCADES):
        picture = combine(kstate).astype(jnp.bfloat16).astype(jnp.float32)
        stored.append(picture)
        model = refine_all(picture, kernel_in[cascade], bias_in[cascade], kernel_out[cascade], bias_out[cascade])
        update = expand(model.astype(jnp.bfloat16))
        kstate = kstate - dc_weight[cascade] * sampled * (kstate - measured) + update
    image_out = combine(kstate)
    adjoint = expand(cotangent)
    grad_measured = jnp.zeros(measured.shape, jnp.float32)
    for cascade in reversed(range(CASCADES)):
        weighted = dc_weight[cascade] * sampled
        grad_measured = grad_measured + weighted * adjoint
        model_bar = combine(adjoint).astype(jnp.bfloat16).astype(jnp.float32)
        adjoint = adjoint - weighted * adjoint

        def local_model(flat, index=cascade):
            return refine_all(flat, kernel_in[index], bias_in[index], kernel_out[index], bias_out[index])
        unused, pull_back = jax.vjp(local_model, stored[cascade])
        picture_bar = pull_back(model_bar)[0]
        adjoint = adjoint + expand(picture_bar.astype(jnp.bfloat16))
    grad_measured = grad_measured + adjoint
    return (image_out, sampled * grad_measured)
```

```python
import functools
import math

import jax
import jax.numpy as jnp
import numpy as np
from jax import lax
from jax.experimental import pallas as pl
from jax.experimental.pallas import tpu as pltpu
from jax.sharding import PartitionSpec as P

BF = jnp.bfloat16
F32 = jnp.float32
HID = 18
WIDE = 384
ROWPAD = 8


def tables(count, wide):
    index = np.arange(count)
    angle = (index[:, None] * index[None, :] % count) * (2.0 * math.pi / count)
    cosine = np.zeros((wide, wide), np.float32)
    sine = np.zeros((wide, wide), np.float32)
    cosine[:count, :count] = np.cos(angle) / math.sqrt(count)
    sine[:count, :count] = np.sin(angle) / math.sqrt(count)
    return cosine, sine


def line_tables(count):
    cosine, sine = tables(count, WIDE)
    return jnp.asarray(cosine).astype(BF), jnp.asarray(sine).astype(BF)


def depth_tables(depth, blocks):
    cosine, sine = tables(depth, depth)
    eye = np.eye(blocks, dtype=np.float32)
    return jnp.asarray(np.kron(eye, cosine)).astype(BF), jnp.asarray(np.kron(eye, sine)).astype(BF)


def dot(a, b):
    return jnp.dot(a, b, preferred_element_type=F32)


def line_transform(real, imag, cosine, sine, sign):
    rows = real.shape[0]
    both = jnp.concatenate([real, imag], axis=0).astype(BF)
    straight = dot(both, cosine)
    crossed = dot(both, sine)
    return straight[:rows] - sign * crossed[rows:], straight[rows:] + sign * crossed[:rows]


def depth_transform(real, imag, cosine, sine, sign):
    both = jnp.concatenate([real, imag], axis=1).astype(BF)
    straight = dot(cosine, both)
    crossed = dot(sine, both)
    return (
        straight[:, :WIDE] - sign * crossed[:, WIDE:],
        straight[:, WIDE:] + sign * crossed[:, :WIDE],
    )


class Row:
    def __init__(self, maps, mask, cosine, sine, zcos, zsin, slots):
        self.maps_real = maps[:, :WIDE].astype(F32)
        self.maps_imag = maps[:, WIDE:].astype(F32)
        self.coils = maps.shape[0] // slots
        self.mask = jnp.concatenate([mask] * self.coils, axis=0)
        self.line = (cosine, sine)
        self.depth = (zcos, zsin)
        self.slots = slots

    def expand(self, picture):
        real = jnp.concatenate([picture[:, :WIDE].astype(F32)] * self.coils, axis=0)
        imag = jnp.concatenate([picture[:, WIDE:].astype(F32)] * self.coils, axis=0)
        out = (
            self.maps_real * real - self.maps_imag * imag,
            self.maps_real * imag + self.maps_imag * real,
        )
        out = line_transform(*out, *self.line, -1.0)
        return depth_transform(*out, *self.depth, -1.0)

    def combine(self, real, imag):
        real, imag = depth_transform(real, imag, *self.depth, 1.0)
        real, imag = line_transform(real, imag, *self.line, 1.0)
        out_real = self.maps_real * real + self.maps_imag * imag
        out_imag = self.maps_real * imag - self.maps_imag * real
        n = self.slots
        return (
            sum(out_real[c * n : c * n + n] for c in range(self.coils)),
            sum(out_imag[c * n : c * n + n] for c in range(self.coils)),
        )

    def normal(self, picture):
        real, imag = self.expand(picture)
        return self.combine(self.mask * real, self.mask * imag)


def start_kernel(weight_ref, k_ref, maps_ref, cot_ref, mask_ref, c_ref, s_ref, zc_ref, zs_ref, y_ref, d_ref):
    slots = cot_ref.shape[0]
    row = Row(maps_ref[...], mask_ref[...], c_ref[...], s_ref[...], zc_ref[...], zs_ref[...], slots)
    weighted = weight_ref[0] * row.mask
    start = []
    for part in (0, 1):
        measured = row.mask * k_ref[:, part * WIDE : part * WIDE + WIDE].astype(F32)
        start.append(measured - weighted * (measured - measured))
    real, imag = row.combine(*start)
    y_ref[:, :WIDE] = real.astype(BF)
    y_ref[:, WIDE:] = imag.astype(BF)
    real, imag = row.normal(cot_ref[...])
    d_ref[:, :WIDE] = real.astype(BF)
    d_ref[:, WIDE:] = imag.astype(BF)


def normal_kernel(maps_ref, pic_ref, mask_ref, c_ref, s_ref, zc_ref, zs_ref, d_ref):
    slots = pic_ref.shape[0]
    row = Row(maps_ref[...], mask_ref[...], c_ref[...], s_ref[...], zc_ref[...], zs_ref[...], slots)
    real, imag = row.normal(pic_ref[...])
    d_ref[:, :WIDE] = real.astype(BF)
    d_ref[:, WIDE:] = imag.astype(BF)


def final_kernel(maps_ref, pic_ref, mask_ref, c_ref, s_ref, zc_ref, zs_ref, g_ref):
    slots = pic_ref.shape[0]
    row = Row(maps_ref[...], mask_ref[...], c_ref[...], s_ref[...], zc_ref[...], zs_ref[...], slots)
    real, imag = row.expand(pic_ref[...])
    g_ref[:, :WIDE] = row.mask * real
    g_ref[:, WIDE:] = row.mask * imag


def shifted(x, down, right):
    if down:
        x = pltpu.roll(x, (-down) % x.shape[0], 0)
    if right:
        x = pltpu.roll(x, (-right) % x.shape[1], 1)
    return x


def rounded(x):
    return x.astype(BF).astype(F32)


def refine_kernel(
    kin_ref, bin_ref, kout_ref, bout_ref, weight_ref,
    y_ref, d_ref, cot_ref, gain_ref, inside_ref,
    m0_ref, total_ref, image_ref,
    taps_ref, hidden_ref, slope_ref,
):
    inside = inside_ref[...]
    gain = gain_ref[...]

    def spread_taps(planes, sign):
        for channel in (0, 1):
            for b in range(3):
                moved = shifted(planes[channel], 0, sign * (b - 1))
                for a in range(3):
                    taps_ref[(a * 3 + b) * 2 + channel] = shifted(moved, sign * (a - 1), 0)

    def gather_taps(sign):
        planes = []
        for channel in (0, 1):
            plane = None
            for b in range(3):
                column = None
                for a in range(3):
                    piece = shifted(taps_ref[(a * 3 + b) * 2 + channel], sign * (a - 1), 0)
                    column = piece if column is None else column + piece
                column = shifted(column, 0, sign * (b - 1))
                plane = column if plane is None else plane + column
            planes.append(plane)
        return planes

    def mix(source_ref, weight_of, first):
        total = first
        for k in range(HID):
            term = weight_of(k) * source_ref[k]
            total = term if total is None else total + term
        return total

    def into_hidden(t, o, k):
        return kin_ref[((t * 9 + k // 2) * HID + o) * 2 + k % 2]

    def out_of_hidden(t, k, o):
        return kout_ref[(t * 18 + k) * HID + o]

    def refine(t, planes):
        spread_taps(planes, 1)

        @pl.loop(0, HID)
        def _(o):
            first = jnp.full(inside.shape, bin_ref[t * HID + o], F32)
            pre = mix(taps_ref, lambda k: into_hidden(t, o, k), first)
            gate = jax.nn.sigmoid(pre)
            hidden_ref[o] = inside * pre * gate
            slope_ref[t, o] = inside * gate * (1.0 + pre * (1.0 - gate))

        @pl.loop(0, HID)
        def _(k):
            taps_ref[k] = mix(hidden_ref, lambda o: out_of_hidden(t, k, o), None)

        planes = gather_taps(1)
        return [rounded(planes[i] + bout_ref[t * 2 + i]) for i in (0, 1)]

    def pull_back(t, planes):
        spread_taps(planes, -1)

        @pl.loop(0, HID)
        def _(o):
            hidden_ref[o] = slope_ref[t, o] * mix(taps_ref, lambda k: out_of_hidden(t, k, o), None)

        @pl.loop(0, HID)
        def _(k):
            channel = lax.rem(k, 2)
            base = (t * 9 + lax.div(k, 2)) * HID
            taps_ref[k] = mix(hidden_ref, lambda o: kin_ref[(base + o) * 2 + channel], None)

        return [rounded(x) for x in gather_taps(-1)]

    def planes_of(ref):
        return [ref[:, :WIDE].astype(F32), ref[:, WIDE:].astype(F32)]

    combined = planes_of(y_ref)
    m0 = refine(0, [rounded(x) for x in combined])
    for i in (0, 1):
        m0_ref[:, i * WIDE : i * WIDE + WIDE] = m0[i].astype(BF)
    state = [combined[i] + gain * m0[i] for i in (0, 1)]
    m1 = refine(1, [rounded(x) for x in state])
    for i in (0, 1):
        image_ref[:, i * WIDE : i * WIDE + WIDE] = state[i] + gain * m1[i]
    cot = planes_of(cot_ref)
    ubar1 = pull_back(1, [rounded(gain * x) for x in cot])
    normal = planes_of(d_ref)
    w0 = weight_ref[0]
    w1 = weight_ref[1]
    mbar0 = [gain * cot[i] - w1 * normal[i] + gain * ubar1[i] for i in (0, 1)]
    ubar0 = pull_back(0, [rounded(x) for x in mbar0])
    kept = w0 + (1.0 - w0)
    for i in (0, 1):
        total = (w1 + kept * (1.0 - w1)) * cot[i] + kept * ubar1[i] + ubar0[i]
        total_ref[:, i * WIDE : i * WIDE + WIDE] = total.astype(BF)


VMEM = pl.BlockSpec(memory_space=pltpu.VMEM)
SMEM = pl.BlockSpec(memory_space=pltpu.SMEM)


def padded(x):
    half = x.shape[-1] // 2
    widths = ((0, 0),) * (x.ndim - 1) + ((0, WIDE - half),)
    return jnp.concatenate([jnp.pad(x[..., :half], widths), jnp.pad(x[..., half:], widths)], axis=-1)


def unpadded(x, half):
    return jnp.concatenate([x[..., :half], x[..., WIDE : WIDE + half]], axis=-1)


def body(kspace, coil_maps, sampling, dc_weight, kernel_in, bias_in, kernel_out, bias_out, cotangent):
    coils, slots, _, width_two = kspace.shape
    rows = coil_maps.shape[2]
    half = width_two // 2
    volumes, depth, _ = sampling.shape
    coil_parts = lax.axis_size("coil")

    cosine, sine = line_tables(half)
    zcos, zsin = depth_tables(depth, volumes * coils)
    fixed = (cosine, sine, zcos, zsin)
    mask = jnp.pad(sampling.astype(F32).reshape(slots, half), ((0, 0), (0, WIDE - half)))
    maps_slice = padded(coil_maps[:, 0])
    cot_slice = padded(cotangent[0])
    k_row = padded(kspace.reshape(coils * slots, width_two))

    def to_rows(x):
        return lax.all_to_all(x, "section", split_axis=1, concat_axis=1, tiled=True)

    def sum_coils(x):
        n = coil_parts
        parts = lax.all_to_all(x.reshape(n, rows // n, x.shape[1]), "coil", 0, 0, tiled=True)
        own = jnp.sum(parts.astype(F32), axis=0).astype(BF)
        spread = jnp.broadcast_to(own[None], (n,) + own.shape)
        return lax.all_to_all(spread, "coil", 0, 0, tiled=True).reshape(x.shape)

    moved = to_rows(jnp.concatenate([maps_slice, cot_slice[None]], axis=0))
    maps_row = moved[:coils].reshape(coils * slots, 2 * WIDE)
    cot_row = moved[coils]

    out_row = jax.ShapeDtypeStruct((slots, 2 * WIDE), BF)
    y_row, d_row = pl.pallas_call(
        start_kernel,
        out_shape=(out_row, out_row),
        in_specs=[SMEM] + [VMEM] * 8,
        out_specs=(VMEM, VMEM),
        name="start",
    )(dc_weight, k_row, maps_row, cot_row, mask, *fixed)

    maps32 = maps_slice.astype(F32)
    gain = jnp.sum(maps32[..., :WIDE] ** 2 + maps32[..., WIDE:] ** 2, axis=0).astype(BF)
    moved = to_rows(jnp.stack([y_row, d_row]))
    sums = sum_coils(jnp.concatenate([moved[0], moved[1], gain], axis=1))
    sums = jnp.pad(sums, ((0, ROWPAD), (0, 0)))
    high = rows + ROWPAD
    inside = np.zeros((high, WIDE), np.float32)
    inside[:rows, :half] = 1.0

    out_slice = jax.ShapeDtypeStruct((high, 2 * WIDE), BF)
    hidden = pltpu.VMEM((HID, high, WIDE), F32)
    m0, total, image = pl.pallas_call(
        refine_kernel,
        out_shape=(out_slice, out_slice, jax.ShapeDtypeStruct((high, 2 * WIDE), F32)),
        in_specs=[SMEM] * 5 + [VMEM] * 5,
        out_specs=(VMEM,) * 3,
        scratch_shapes=[hidden, hidden, pltpu.VMEM((2, HID, high, WIDE), F32)],
        name="refine",
    )(
        kernel_in.reshape(-1), bias_in.reshape(-1), kernel_out.reshape(-1), bias_out.reshape(-1), dc_weight,
        sums[:, : 2 * WIDE], sums[:, 2 * WIDE : 4 * WIDE],
        jnp.pad(cot_slice, ((0, ROWPAD), (0, 0))), sums[:, 4 * WIDE :].astype(F32), jnp.asarray(inside),
    )

    total_row = to_rows(total[None, :rows])[0]
    grad = pl.pallas_call(
        final_kernel,
        out_shape=jax.ShapeDtypeStruct((coils * slots, 2 * WIDE), F32),
        in_specs=[VMEM] * 7,
        out_specs=VMEM,
        name="final",
    )(maps_row, total_row, mask, *fixed)

    m0_row = to_rows(m0[None, :rows])[0]
    d0_row = pl.pallas_call(
        normal_kernel,
        out_shape=out_row,
        in_specs=[VMEM] * 7,
        out_specs=VMEM,
        name="normal",
    )(maps_row, m0_row, mask, *fixed)
    d0 = sum_coils(to_rows(d0_row[None])[0]).astype(F32)
    image = image[:rows] - dc_weight[1] * d0
    return (
        unpadded(image, half)[None],
        unpadded(grad, half).reshape(coils, slots, 1, width_two),
    )


def solution(mesh):
    return jax.shard_map(
        body,
        mesh=mesh,
        in_specs=(
            P("coil", None, "section", None),
            P("coil", "section", None, None),
            P(), P(), P(), P(), P(), P(),
            P("section", None, None),
        ),
        out_specs=(P("section", None, None), P("coil", None, "section", None)),
        check_vma=False,
    )
```

```python
import functools
import math

import jax
import jax.numpy as jnp
import numpy as np
from jax import lax
from jax.experimental import pallas as pl
from jax.experimental.pallas import tpu as pltpu
from jax.sharding import PartitionSpec as P

BF = jnp.bfloat16
F32 = jnp.float32
HID = 18
WIDE = 384
HALO = 8


def tables(count, wide):
    index = np.arange(count)
    angle = (index[:, None] * index[None, :] % count) * (2.0 * math.pi / count)
    cosine = np.zeros((wide, wide), np.float32)
    sine = np.zeros((wide, wide), np.float32)
    cosine[:count, :count] = np.cos(angle) / math.sqrt(count)
    sine[:count, :count] = np.sin(angle) / math.sqrt(count)
    return cosine, sine


def line_tables(count):
    cosine, sine = tables(count, WIDE)
    return jnp.asarray(cosine).astype(BF), jnp.asarray(sine).astype(BF)


def depth_tables(depth, blocks):
    cosine, sine = tables(depth, depth)
    eye = np.eye(blocks, dtype=np.float32)
    return jnp.asarray(np.kron(eye, cosine)).astype(BF), jnp.asarray(np.kron(eye, sine)).astype(BF)


def dot(a, b):
    return jnp.dot(a, b, preferred_element_type=F32)


def line_transform(real, imag, cosine, sine, sign):
    rows = real.shape[0]
    both = jnp.concatenate([real, imag], axis=0).astype(BF)
    straight = dot(both, cosine)
    crossed = dot(both, sine)
    return straight[:rows] - sign * crossed[rows:], straight[rows:] + sign * crossed[:rows]


def depth_transform(real, imag, cosine, sine, sign):
    both = jnp.concatenate([real, imag], axis=1).astype(BF)
    straight = dot(cosine, both)
    crossed = dot(sine, both)
    return (
        straight[:, :WIDE] - sign * crossed[:, WIDE:],
        straight[:, WIDE:] + sign * crossed[:, :WIDE],
    )


class Row:
    def __init__(self, mask, line, depth):
        self.mask = mask
        self.line = line
        self.depth = depth

    def take_maps(self, planes):
        self.coils = planes.shape[0] // 2
        self.maps_real = jnp.concatenate([planes[2 * i] for i in range(self.coils)], axis=0)
        self.maps_imag = jnp.concatenate([planes[2 * i + 1] for i in range(self.coils)], axis=0)

    def expand(self, picture):
        real = jnp.concatenate([picture[0]] * self.coils, axis=0)
        imag = jnp.concatenate([picture[1]] * self.coils, axis=0)
        out = (
            self.maps_real * real - self.maps_imag * imag,
            self.maps_real * imag + self.maps_imag * real,
        )
        out = line_transform(*out, *self.line, -1.0)
        return depth_transform(*out, *self.depth, -1.0)

    def inverse(self, real, imag):
        real, imag = depth_transform(real, imag, *self.depth, 1.0)
        return line_transform(real, imag, *self.line, 1.0)

    def collect(self, real, imag):
        out_real = self.maps_real * real + self.maps_imag * imag
        out_imag = self.maps_real * imag - self.maps_imag * real
        n = out_real.shape[0] // self.coils
        return [
            sum(out[i * n : i * n + n] for i in range(self.coils)) for out in (out_real, out_imag)
        ]

    def normal(self, picture):
        real, imag = self.expand(picture)
        return self.collect(*self.inverse(self.mask * real, self.mask * imag))


def shifted(x, down, right):
    if down:
        x = pltpu.roll(x, (-down) % x.shape[0], 0)
    if right:
        x = pltpu.roll(x, (-right) % x.shape[1], 1)
    return x


def rounded(x):
    return x.astype(BF).astype(F32)


class Refiner:
    def __init__(self, kin_ref, bin_ref, kout_ref, bout_ref, inside, taps_ref, hidden_ref, slope_ref):
        self.kin, self.bin, self.kout, self.bout = kin_ref, bin_ref, kout_ref, bout_ref
        self.inside = inside
        self.taps, self.hidden, self.slope = taps_ref, hidden_ref, slope_ref

    def spread_taps(self, planes, sign):
        for channel in (0, 1):
            for b in range(3):
                moved = shifted(planes[channel], 0, sign * (b - 1))
                for a in range(3):
                    self.taps[(a * 3 + b) * 2 + channel] = shifted(moved, sign * (a - 1), 0)

    def gather_taps(self, sign):
        planes = []
        for channel in (0, 1):
            plane = None
            for b in range(3):
                column = None
                for a in range(3):
                    piece = shifted(self.taps[(a * 3 + b) * 2 + channel], sign * (a - 1), 0)
                    column = piece if column is None else column + piece
                column = shifted(column, 0, sign * (b - 1))
                plane = column if plane is None else plane + column
            planes.append(plane)
        return planes

    @staticmethod
    def mix(source_ref, weight_of, first):
        total = first
        for k in range(HID):
            term = weight_of(k) * source_ref[k]
            total = term if total is None else total + term
        return total

    def into_hidden(self, t, o, k):
        return self.kin[((t * 9 + k // 2) * HID + o) * 2 + k % 2]

    def out_of_hidden(self, t, k, o):
        return self.kout[(t * 18 + k) * HID + o]

    def refine(self, t, planes):
        self.spread_taps(planes, 1)

        @pl.loop(0, HID)
        def _(o):
            first = jnp.full(self.inside.shape, self.bin[t * HID + o], F32)
            pre = self.mix(self.taps, lambda k: self.into_hidden(t, o, k), first)
            gate = jax.nn.sigmoid(pre)
            self.hidden[o] = self.inside * pre * gate
            self.slope[t, o] = self.inside * gate * (1.0 + pre * (1.0 - gate))

        @pl.loop(0, HID)
        def _(k):
            self.taps[k] = self.mix(self.hidden, lambda o: self.out_of_hidden(t, k, o), None)

        planes = self.gather_taps(1)
        return [rounded(planes[i] + self.bout[t * 2 + i]) for i in (0, 1)]

    def pull_back(self, t, planes):
        self.spread_taps(planes, -1)

        @pl.loop(0, HID)
        def _(o):
            self.hidden[o] = self.slope[t, o] * self.mix(
                self.taps, lambda k: self.out_of_hidden(t, k, o), None
            )

        @pl.loop(0, HID)
        def _(k):
            channel = lax.rem(k, 2)
            base = (t * 9 + lax.div(k, 2)) * HID
            self.taps[k] = self.mix(self.hidden, lambda o: self.kin[(base + o) * 2 + channel], None)

        return [rounded(x) for x in self.gather_taps(-1)]


def clear(first_ref, second_ref, side):
    first_ref[side] = jnp.zeros(first_ref.shape[1:], first_ref.dtype)
    second_ref[side] = jnp.zeros(second_ref.shape[1:], second_ref.dtype)


def cascade_kernel(
    parts, coil_parts,
    kin_ref, bin_ref, kout_ref, bout_ref, weight_ref,
    k_ref, maps_ref, cot_ref, gain_ref, window_ref, inside_ref, mask_ref,
    c_ref, s_ref, zc_ref, zs_ref,
    image_ref, grad_ref,
    maps_row, cot_row, gain_all,
    y_src, y_dst, d_src, d_dst, e_src, e_dst,
    edge_src, edge_dst, edge2_src, edge2_dst, win,
    m_src, m_dst, t_src, t_dst, image_src, image_dst, state_ref, ubar_ref,
    taps_ref, hidden_ref, slope_ref,
    send, recv, edge_send, edge_recv,
):
    rows = maps_ref.shape[0]
    columns = coil_parts // 2
    block = rows // columns
    me_s = lax.axis_index("section")
    me_c = lax.axis_index("coil")
    me_x = lax.rem(me_c, columns)
    me_hi = lax.div(me_c, columns)
    my_block = lax.div(me_s, block)
    active = me_hi == lax.rem(me_s, 2)
    to_self = jnp.logical_and(active, me_x == my_block)

    def holder(slot, x):
        return lax.rem(slot, 2) * columns + x

    def whenever(condition, yes, no=None):
        pl.when(condition)(yes)
        if no is not None:
            pl.when(jnp.logical_not(condition))(no)

    def push(index, src, dst, section, coil):
        mine = jnp.logical_and(section == me_s, coil == me_c)

        def near():
            pltpu.make_async_copy(src, dst, recv.at[index]).start()

        def far():
            pltpu.make_async_remote_copy(
                src, dst, send.at[index], recv.at[index],
                device_id={"section": section, "coil": coil}, device_id_type=pl.DeviceIdType.MESH,
            ).start()

        whenever(mine, near, far)

    def arrived(index, ref):
        pltpu.make_async_copy(ref, ref, recv.at[index]).wait()

    def left(index, ref):
        pltpu.make_async_copy(ref, ref, send.at[index]).wait()

    barrier = pltpu.get_barrier_semaphore()

    def greet(section, coil):
        def signal():
            pl.semaphore_signal(
                barrier, 1, device_id={"section": section, "coil": coil}, device_id_type=pl.DeviceIdType.MESH
            )

        mine = jnp.logical_and(section == me_s, coil == me_c)
        pl.when(jnp.logical_not(mine))(signal)

    @pl.loop(0, parts)
    def _(p):
        greet(p, me_c)
        greet(p, holder(p, my_block))

    @pl.loop(0, columns)
    def _(x):
        greet(me_s, holder(me_s, x))

    @pl.when(active)
    def _():
        @pl.loop(0, block)
        def _(i):
            @pl.loop(0, coil_parts)
            def _(q):
                greet(me_x * block + i, q)

        @pl.loop(0, coil_parts)
        def _(q):
            greet(me_s, q)

        pl.when(me_x > 0)(lambda: greet(me_s, me_c - 1))
        pl.when(me_x < columns - 1)(lambda: greet(me_s, me_c + 1))

    one = jnp.int32(1)
    zero = jnp.int32(0)
    act = jnp.where(active, one, zero)
    own = jnp.where(to_self, one, zero)
    sides = jnp.where(me_x > 0, one, zero) + jnp.where(me_x < columns - 1, one, zero)
    expected = (
        (parts - 1) + (parts - own) + (columns - act)
        + act * (block * coil_parts - own + (coil_parts - 1) + sides)
    )
    pl.semaphore_wait(barrier, expected)

    @pl.loop(0, parts)
    def _(k):
        p = lax.rem(me_s + k, parts)
        push(0, maps_ref.at[p], maps_row.at[me_s], p, me_c)

    @pl.loop(0, columns)
    def _(x):
        push(1, gain_ref.at[x], gain_all.at[me_c], me_s, holder(me_s, x))

    @pl.loop(0, parts)
    def _(k):
        p = lax.rem(me_s + k, parts)
        push(2, cot_ref.at[p], cot_row.at[me_s], p, me_c)

    pl.when(me_x == 0)(lambda: clear(edge_dst, edge2_dst, 0))
    pl.when(me_x == columns - 1)(lambda: clear(edge_dst, edge2_dst, 1))

    def to_holders(index, src, dst):
        place = me_c * block + lax.rem(me_s, block)

        @pl.loop(0, parts)
        def _(k):
            p = lax.rem(me_s + k, parts)
            push(index, src.at[p], dst.at[place], p, holder(p, my_block))

    def to_owners(index, src, dst):
        @pl.loop(0, block)
        def _(i):
            @pl.loop(0, coil_parts)
            def _(q):
                push(index, src.at[i], dst.at[me_s], me_x * block + i, q)

    def slots_of(ref):
        return jnp.swapaxes(ref[...].astype(F32), 0, 1)

    def summed(ref):
        all_parts = ref[...].astype(F32)
        total = all_parts[:block]
        for q in range(1, coil_parts):
            total = total + all_parts[q * block : q * block + block]
        return jnp.swapaxes(total, 0, 1)

    mask = mask_ref[...]
    coils = k_ref.shape[0] // mask.shape[0]
    row = Row(
        jnp.concatenate([mask] * coils, axis=0),
        (c_ref[...], s_ref[...]), (zc_ref[...], zs_ref[...]),
    )
    weighted = weight_ref[0] * row.mask
    start = []
    for part in (0, 1):
        measured = row.mask * k_ref[:, part * WIDE : part * WIDE + WIDE].astype(F32)
        start.append(measured - weighted * (measured - measured))
    images = row.inverse(*start)
    arrived(0, maps_row)
    row.take_maps(slots_of(maps_row))
    y_src[...] = jnp.stack(row.collect(*images), axis=1).astype(BF)
    to_holders(3, y_src, y_dst)
    arrived(2, cot_row)
    d_src[...] = jnp.stack(row.normal(slots_of(cot_row)), axis=1).astype(BF)
    to_holders(4, d_src, d_dst)

    def exchange_edges(which, src, dst, count):
        def link(side, coil):
            return pltpu.make_async_remote_copy(
                src.at[side], dst.at[1 - side],
                edge_send.at[which * 2 + side], edge_recv.at[which * 2 + 1 - side],
                device_id={"section": me_s, "coil": coil}, device_id_type=pl.DeviceIdType.MESH,
            )

        def coming(side):
            pltpu.make_async_copy(dst.at[side], dst.at[side], edge_recv.at[which * 2 + side]).wait()

        pl.when(me_x > 0)(lambda: link(0, me_c - 1).start())
        pl.when(me_x < columns - 1)(lambda: link(1, me_c + 1).start())
        pl.when(me_x > 0)(lambda: coming(0))
        pl.when(me_x < columns - 1)(lambda: coming(1))

    def open_window(first, planes, which, src, dst):
        for i, plane in enumerate(planes):
            plane = rounded(plane)
            win[first + i, HALO : HALO + block] = plane
            src[0, i] = plane[:HALO].astype(BF)
            src[1, i] = plane[block - HALO :].astype(BF)
        exchange_edges(which, src, dst, len(planes))
        for i in range(len(planes)):
            win[first + i, :HALO] = dst[0, i].astype(F32)
            win[first + i, HALO + block :] = dst[1, i].astype(F32)

    inner = slice(HALO, HALO + block)

    @pl.when(active)
    def _():
        net = Refiner(
            kin_ref, bin_ref, kout_ref, bout_ref, inside_ref[...], taps_ref, hidden_ref, slope_ref
        )
        arrived(1, gain_all)
        gains = jnp.sum(gain_all[...].astype(F32), axis=0)
        arrived(3, y_dst)
        total = summed(y_dst)
        open_window(0, [total[0], total[1], gains], 0, edge_src, edge_dst)
        gain = win[2]
        m0 = net.refine(0, [rounded(win[0]), rounded(win[1])])
        m_src[...] = jnp.stack([m0[0][inner], m0[1][inner]], axis=1).astype(BF)
        to_owners(5, m_src, m_dst)
        for i in (0, 1):
            state_ref[i] = win[i] + gain * m0[i]
        m1 = net.refine(1, [rounded(state_ref[0]), rounded(state_ref[1])])
        for i in (0, 1):
            state_ref[i] = state_ref[i] + gain * m1[i]
        ubar1 = net.pull_back(1, [rounded(gain * window_ref[i].astype(F32)) for i in (0, 1)])
        for i in (0, 1):
            ubar_ref[i] = ubar1[i]
        arrived(4, d_dst)
        total = summed(d_dst)
        open_window(3, [total[0], total[1]], 1, edge2_src, edge2_dst)
        w0 = weight_ref[0]
        w1 = weight_ref[1]
        mbar0 = [
            rounded(gain * window_ref[i].astype(F32) - w1 * win[3 + i] + gain * ubar_ref[i]) for i in (0, 1)
        ]
        ubar0 = net.pull_back(0, mbar0)
        kept = w0 + (1.0 - w0)
        out = [
            (w1 + kept * (1.0 - w1)) * window_ref[i].astype(F32) + kept * ubar_ref[i] + ubar0[i]
            for i in (0, 1)
        ]
        t_src[...] = jnp.stack([out[0][inner], out[1][inner]], axis=1).astype(BF)
        to_owners(6, t_src, t_dst)

    arrived(5, m_dst)
    e_src[...] = jnp.stack(row.normal(slots_of(m_dst)), axis=1).astype(BF)
    to_holders(7, e_src, e_dst)
    arrived(6, t_dst)
    real, imag = row.expand(slots_of(t_dst))
    grad_ref[:, :WIDE] = row.mask * real
    grad_ref[:, WIDE:] = row.mask * imag

    @pl.when(active)
    def _():
        arrived(7, e_dst)
        total = summed(e_dst)
        for i in (0, 1):
            image_src[0, i] = (state_ref[i, inner] - weight_ref[1] * total[i]).astype(BF)

        @pl.loop(0, coil_parts)
        def _(q):
            push(8, image_src.at[0], image_dst.at[me_x], me_s, q)

    arrived(8, image_dst)
    for x in range(columns):
        for i in (0, 1):
            image_ref[i, x * block : x * block + block] = image_dst[x, i].astype(F32)

    left(0, maps_ref.at[pl.ds(0, parts - 1)])
    left(2, cot_ref.at[pl.ds(0, parts - 1)])
    if columns > 1:
        whenever(active, lambda: left(1, gain_ref.at[pl.ds(0, columns - 1)]), lambda: left(1, gain_ref))
    else:
        pl.when(jnp.logical_not(active))(lambda: left(1, gain_ref))
    for index, src in ((3, y_src), (4, d_src), (7, e_src)):
        whenever(
            to_self,
            functools.partial(left, index, src.at[pl.ds(0, parts - 1)]),
            functools.partial(left, index, src),
        )

    @pl.when(active)
    def _():
        for index, like in ((5, e_dst), (6, e_dst)):
            whenever(
                to_self,
                functools.partial(left, index, like.at[pl.ds(0, block * coil_parts - 1)]),
                functools.partial(left, index, like),
            )
        left(8, image_src)
        for which, src in ((0, edge_src), (1, edge2_src)):
            for side, there in ((0, me_x > 0), (1, me_x < columns - 1)):
                def gone(which=which, side=side, src=src):
                    pltpu.make_async_copy(
                        src.at[side], src.at[side], edge_send.at[which * 2 + side]
                    ).wait()

                pl.when(there)(gone)


VMEM = pl.BlockSpec(memory_space=pltpu.VMEM)
SMEM = pl.BlockSpec(memory_space=pltpu.SMEM)


def planes_last(x):
    half = x.shape[-1] // 2
    x = x.reshape(x.shape[:-1] + (2, half))
    return jnp.pad(x, ((0, 0),) * (x.ndim - 1) + ((0, WIDE - half),))


def body(kspace, coil_maps, sampling, dc_weight, kernel_in, bias_in, kernel_out, bias_out, cotangent):
    coils, slots, _, width_two = kspace.shape
    rows = coil_maps.shape[2]
    half = width_two // 2
    volumes, depth, _ = sampling.shape
    coil_parts = lax.axis_size("coil")
    parts = lax.axis_size("section")
    columns = coil_parts // 2
    block = rows // columns
    high = block + 2 * HALO
    me_x = lax.rem(lax.axis_index("coil"), columns)

    cosine, sine = line_tables(half)
    zcos, zsin = depth_tables(depth, volumes * coils)
    mask = jnp.pad(sampling.astype(F32).reshape(slots, half), ((0, 0), (0, WIDE - half)))
    k_row = planes_last(kspace.reshape(coils * slots, width_two)).reshape(coils * slots, 2 * WIDE)
    maps_out = planes_last(jnp.swapaxes(coil_maps[:, 0], 0, 1)).reshape(rows, 2 * coils, WIDE)
    cot_out = planes_last(cotangent[0])
    gain = jnp.sum(maps_out.astype(F32) ** 2, axis=1).astype(BF).reshape(columns, block, WIDE)
    first = me_x * block
    window = lax.dynamic_slice_in_dim(
        jnp.pad(jnp.swapaxes(cot_out, 0, 1), ((0, 0), (HALO, HALO), (0, 0))), first, high, axis=1
    )
    place = first - HALO + lax.broadcasted_iota(jnp.int32, (high, WIDE), 0)
    line = lax.broadcasted_iota(jnp.int32, (high, WIDE), 1)
    inside = ((place >= 0) & (place < rows) & (line < half)).astype(F32)

    pair = pltpu.VMEM((slots, 2, WIDE), BF)
    gathered = pltpu.VMEM((coil_parts * block, 2, WIDE), BF)
    owned = pltpu.VMEM((block, 2, WIDE), BF)
    plane2 = pltpu.VMEM((2, high, WIDE), F32)
    hidden = pltpu.VMEM((HID, high, WIDE), F32)
    image, grad = pl.pallas_call(
        functools.partial(cascade_kernel, parts, coil_parts),
        out_shape=(
            jax.ShapeDtypeStruct((2, rows, WIDE), F32),
            jax.ShapeDtypeStruct((coils * slots, 2 * WIDE), F32),
        ),
        in_specs=[SMEM] * 5 + [VMEM] * 11,
        out_specs=(VMEM, VMEM),
        scratch_shapes=[
            pltpu.VMEM((slots, 2 * coils, WIDE), BF),
            pair,
            pltpu.VMEM((coil_parts, block, WIDE), BF),
            pair, gathered, pair, gathered, pair, gathered,
            pltpu.VMEM((2, 3, HALO, WIDE), BF), pltpu.VMEM((2, 3, HALO, WIDE), BF),
            pltpu.VMEM((2, 2, HALO, WIDE), BF), pltpu.VMEM((2, 2, HALO, WIDE), BF),
            pltpu.VMEM((5, high, WIDE), F32),
            owned, pair, owned, pair,
            pltpu.VMEM((coil_parts - 1, 2, block, WIDE), BF),
            pltpu.VMEM((columns, 2, block, WIDE), BF),
            plane2, plane2,
            hidden, hidden, pltpu.VMEM((2, HID, high, WIDE), F32),
            pltpu.SemaphoreType.DMA((9,)), pltpu.SemaphoreType.DMA((9,)),
            pltpu.SemaphoreType.DMA((4,)), pltpu.SemaphoreType.DMA((4,)),
        ],
        compiler_params=pltpu.CompilerParams(collective_id=0, has_side_effects=True),
        name="cascade",
    )(
        kernel_in.reshape(-1), bias_in.reshape(-1), kernel_out.reshape(-1), bias_out.reshape(-1), dc_weight,
        k_row, maps_out, cot_out, gain, window, inside, mask, cosine, sine, zcos, zsin,
    )
    image = jnp.concatenate([image[0, :, :half], image[1, :, :half]], axis=-1)
    grad = jnp.concatenate([grad[:, :half], grad[:, WIDE : WIDE + half]], axis=-1)
    return image[None], grad.reshape(coils, slots, 1, width_two)


def solution(mesh):
    return jax.shard_map(
        body,
        mesh=mesh,
        in_specs=(
            P("coil", None, "section", None),
            P("coil", "section", None, None),
            P(), P(), P(), P(), P(), P(),
            P("section", None, None),
        ),
        out_specs=(P("section", None, None), P("coil", None, "section", None)),
        check_vma=False,
    )
```

```python
import functools
import math

import jax
import jax.numpy as jnp
import numpy as np
from jax import lax
from jax.experimental import pallas as pl
from jax.experimental.pallas import tpu as pltpu
from jax.sharding import PartitionSpec as P

BF = jnp.bfloat16
F32 = jnp.float32
HID = 18
WIDE = 384
HALO = 8


def tables(count, wide):
    index = np.arange(count)
    angle = (index[:, None] * index[None, :] % count) * (2.0 * math.pi / count)
    cosine = np.zeros((wide, wide), np.float32)
    sine = np.zeros((wide, wide), np.float32)
    cosine[:count, :count] = np.cos(angle) / math.sqrt(count)
    sine[:count, :count] = np.sin(angle) / math.sqrt(count)
    return cosine, sine


def line_tables(count):
    cosine, sine = tables(count, WIDE)
    return jnp.asarray(cosine).astype(BF), jnp.asarray(sine).astype(BF)


def depth_tables(depth, blocks):
    cosine, sine = tables(depth, depth)
    eye = np.eye(blocks, dtype=np.float32)
    return jnp.asarray(np.kron(eye, cosine)).astype(BF), jnp.asarray(np.kron(eye, sine)).astype(BF)


def dot(a, b):
    return jnp.dot(a, b, preferred_element_type=F32)


def line_transform(real, imag, cosine, sine, sign):
    rows = real.shape[0]
    both = jnp.concatenate([real, imag], axis=0).astype(BF)
    straight = dot(both, cosine)
    crossed = dot(both, sine)
    return straight[:rows] - sign * crossed[rows:], straight[rows:] + sign * crossed[:rows]


def depth_transform(real, imag, cosine, sine, sign):
    both = jnp.concatenate([real, imag], axis=1).astype(BF)
    straight = dot(cosine, both)
    crossed = dot(sine, both)
    return (
        straight[:, :WIDE] - sign * crossed[:, WIDE:],
        straight[:, WIDE:] + sign * crossed[:, :WIDE],
    )


class Row:
    def __init__(self, mask, line, depth):
        self.mask = mask
        self.line = line
        self.depth = depth

    def take_maps(self, planes):
        self.coils = planes.shape[0]
        stacked = jnp.concatenate([planes[i] for i in range(self.coils)], axis=0)
        self.maps_real, self.maps_imag = planes_of(stacked)

    def expand(self, picture):
        real = jnp.concatenate([picture[0]] * self.coils, axis=0)
        imag = jnp.concatenate([picture[1]] * self.coils, axis=0)
        out = (
            self.maps_real * real - self.maps_imag * imag,
            self.maps_real * imag + self.maps_imag * real,
        )
        out = line_transform(*out, *self.line, -1.0)
        return depth_transform(*out, *self.depth, -1.0)

    def inverse(self, real, imag):
        real, imag = depth_transform(real, imag, *self.depth, 1.0)
        return line_transform(real, imag, *self.line, 1.0)

    def collect(self, real, imag):
        out_real = self.maps_real * real + self.maps_imag * imag
        out_imag = self.maps_real * imag - self.maps_imag * real
        n = out_real.shape[0] // self.coils
        return [
            sum(out[i * n : i * n + n] for i in range(self.coils)) for out in (out_real, out_imag)
        ]

    def normal(self, picture):
        real, imag = self.expand(picture)
        return self.collect(*self.inverse(self.mask * real, self.mask * imag))


def shifted(x, down, right):
    if down:
        x = pltpu.roll(x, (-down) % x.shape[0], 0)
    if right:
        x = pltpu.roll(x, (-right) % x.shape[1], 1)
    return x


def widen(x):
    return jnp.concatenate([x, jnp.zeros((x.shape[0], WIDE - x.shape[1]), x.dtype)], axis=1)


def planes_of(x):
    half = x.shape[1] // 2
    return [widen(x[:, :half].astype(F32)), widen(x[:, half:].astype(F32))]


def packed(planes, half):
    return jnp.concatenate([planes[0][:, :half], planes[1][:, :half]], axis=1)


def rounded(x):
    return x.astype(BF).astype(F32)


class Refiner:
    def __init__(self, kin_ref, bin_ref, kout_ref, bout_ref, inside, taps_ref, hidden_ref, slope_ref):
        self.kin, self.bin, self.kout, self.bout = kin_ref, bin_ref, kout_ref, bout_ref
        self.inside = inside
        self.taps, self.hidden, self.slope = taps_ref, hidden_ref, slope_ref

    def spread_taps(self, planes, sign):
        for channel in (0, 1):
            for b in range(3):
                moved = shifted(planes[channel], 0, sign * (b - 1))
                for a in range(3):
                    self.taps[(a * 3 + b) * 2 + channel] = shifted(moved, sign * (a - 1), 0)

    def gather_taps(self, sign):
        planes = []
        for channel in (0, 1):
            plane = None
            for b in range(3):
                column = None
                for a in range(3):
                    piece = shifted(self.taps[(a * 3 + b) * 2 + channel], sign * (a - 1), 0)
                    column = piece if column is None else column + piece
                column = shifted(column, 0, sign * (b - 1))
                plane = column if plane is None else plane + column
            planes.append(plane)
        return planes

    @staticmethod
    def mix(source_ref, weight_of, first):
        total = first
        for k in range(HID):
            term = weight_of(k) * source_ref[k]
            total = term if total is None else total + term
        return total

    def into_hidden(self, t, o, k):
        return self.kin[t, k // 2, k % 2, o]

    def out_of_hidden(self, t, k, o):
        if isinstance(k, int):
            return self.kout[t, k // 2, k % 2, o]
        return self.kout[t, lax.div(k, 2), lax.rem(k, 2), o]

    def refine(self, t, planes):
        self.spread_taps(planes, 1)

        @pl.loop(0, HID)
        def _(o):
            first = jnp.full(self.inside.shape, self.bin[t, o], F32)
            pre = self.mix(self.taps, lambda k: self.into_hidden(t, o, k), first)
            gate = jax.nn.sigmoid(pre)
            self.hidden[o] = self.inside * pre * gate
            self.slope[t, o] = self.inside * gate * (1.0 + pre * (1.0 - gate))

        @pl.loop(0, HID)
        def _(k):
            self.taps[k] = self.mix(self.hidden, lambda o: self.out_of_hidden(t, k, o), None)

        planes = self.gather_taps(1)
        return [rounded(planes[i] + self.bout[t, i]) for i in (0, 1)]

    def pull_back(self, t, planes):
        self.spread_taps(planes, -1)

        @pl.loop(0, HID)
        def _(o):
            self.hidden[o] = self.slope[t, o] * self.mix(
                self.taps, lambda k: self.out_of_hidden(t, k, o), None
            )

        @pl.loop(0, HID)
        def _(k):
            tap = lax.div(k, 2)
            channel = lax.rem(k, 2)
            self.taps[k] = self.mix(self.hidden, lambda o: self.kin[t, tap, channel, o], None)

        return [rounded(x) for x in self.gather_taps(-1)]


def clear(first_ref, second_ref, side):
    first_ref[side] = jnp.zeros(first_ref.shape[1:], first_ref.dtype)
    second_ref[side] = jnp.zeros(second_ref.shape[1:], second_ref.dtype)


def cascade_kernel(
    parts, coil_parts,
    kin_ref, bin_ref, kout_ref, bout_ref, weight_ref,
    maps_any, cot_any, sampling_any, k_any, c_any, s_any, zc_any, zs_any,
    image_ref, grad_ref,
    maps_in, cot_in, sampling_in, k_ref, c_ref, s_ref, zc_ref, zs_ref, load,
    maps_ref, cot_ref, gain_ref, cot_pad,
    maps_row, cot_row, gain_all,
    y_src, y_dst, d_src, d_dst, e_src, e_dst,
    edge_src, edge_dst, edge2_src, edge2_dst, win,
    m_src, m_dst, t_src, t_dst, image_src, image_dst, state_ref, ubar_ref,
    taps_ref, hidden_ref, slope_ref,
    send, recv, edge_send, edge_recv,
):
    rows = maps_ref.shape[0]
    half = sampling_in.shape[1]
    columns = coil_parts // 2
    block = rows // columns
    me_s = lax.axis_index("section")
    me_c = lax.axis_index("coil")
    me_x = lax.rem(me_c, columns)
    me_hi = lax.div(me_c, columns)
    my_block = lax.div(me_s, block)
    active = me_hi == lax.rem(me_s, 2)
    to_self = jnp.logical_and(active, me_x == my_block)

    def holder(slot, x):
        return lax.rem(slot, 2) * columns + x

    def whenever(condition, yes, no=None):
        pl.when(condition)(yes)
        if no is not None:
            pl.when(jnp.logical_not(condition))(no)

    def push(index, src, dst, section, coil):
        mine = jnp.logical_and(section == me_s, coil == me_c)

        def near():
            pltpu.make_async_copy(src, dst, recv.at[index]).start()

        def far():
            pltpu.make_async_remote_copy(
                src, dst, send.at[index], recv.at[index],
                device_id={"section": section, "coil": coil}, device_id_type=pl.DeviceIdType.MESH,
            ).start()

        whenever(mine, near, far)

    def arrived(index, ref):
        pltpu.make_async_copy(ref, ref, recv.at[index]).wait()

    def left(index, ref):
        pltpu.make_async_copy(ref, ref, send.at[index]).wait()

    barrier = pltpu.get_barrier_semaphore()

    def greet(section, coil):
        pl.semaphore_signal(
            barrier, 1, device_id={"section": section, "coil": coil}, device_id_type=pl.DeviceIdType.MESH
        )

    @pl.loop(1, parts)
    def _(k):
        greet(lax.rem(me_s + k, parts), me_c)

    @pl.loop(1, coil_parts)
    def _(k):
        greet(me_s, lax.rem(me_c + k, coil_parts))

    loads = [
        pltpu.make_async_copy(src, dst, load.at[i])
        for i, (src, dst) in enumerate(
            zip(
                (maps_any, cot_any, sampling_any, k_any, c_any, s_any, zc_any, zs_any),
                (maps_in, cot_in, sampling_in, k_ref, c_ref, s_ref, zc_ref, zs_ref),
            )
        )
    ]
    for copy in loads:
        copy.start()

    loads[0].wait()
    maps_ref[...] = jnp.swapaxes(maps_in[...], 0, 1)
    gain = None
    for i in range(maps_in.shape[0]):
        for plane in planes_of(maps_in[i]):
            gain = plane * plane if gain is None else gain + plane * plane
    for x in range(columns):
        gain_ref[x] = gain[x * block : x * block + block].astype(BF)
    loads[1].wait()
    cot_planes = planes_of(cot_in[...])
    cot_ref[...] = jnp.stack(cot_planes, axis=1).astype(BF)
    for i in (0, 1):
        cot_pad[i, :HALO] = jnp.zeros((HALO, WIDE), F32)
        cot_pad[i, HALO + rows :] = jnp.zeros((HALO, WIDE), F32)
        cot_pad[i, HALO : HALO + rows] = cot_planes[i]
    high = block + 2 * HALO
    first_row = pl.multiple_of(me_x * block, HALO)
    window = [cot_pad[i, pl.ds(first_row, high), :] for i in (0, 1)]
    place = first_row - HALO + lax.broadcasted_iota(jnp.int32, (high, WIDE), 0)
    line = lax.broadcasted_iota(jnp.int32, (high, WIDE), 1)
    inside = jnp.where((place >= 0) & (place < rows) & (line < half), 1.0, 0.0).astype(F32)
    loads[2].wait()
    mask = widen(sampling_in[...].astype(F32))

    pl.semaphore_wait(barrier, parts - 1 + coil_parts - 1)

    @pl.loop(0, parts)
    def _(k):
        p = lax.rem(me_s + k, parts)
        push(0, maps_ref.at[p], maps_row.at[me_s], p, me_c)

    @pl.loop(0, columns)
    def _(x):
        push(1, gain_ref.at[x], gain_all.at[me_c], me_s, holder(me_s, x))

    @pl.loop(0, parts)
    def _(k):
        p = lax.rem(me_s + k, parts)
        push(2, cot_ref.at[p], cot_row.at[me_s], p, me_c)

    pl.when(me_x == 0)(lambda: clear(edge_dst, edge2_dst, 0))
    pl.when(me_x == columns - 1)(lambda: clear(edge_dst, edge2_dst, 1))

    def to_holders(index, src, dst):
        place = me_c * block + lax.rem(me_s, block)

        @pl.loop(0, parts)
        def _(k):
            p = lax.rem(me_s + k, parts)
            push(index, src.at[p], dst.at[place], p, holder(p, my_block))

    def to_owners(index, src, dst):
        @pl.loop(0, block)
        def _(i):
            @pl.loop(0, coil_parts)
            def _(q):
                push(index, src.at[i], dst.at[me_s], me_x * block + i, q)

    def slots_of(ref):
        return jnp.swapaxes(ref[...].astype(F32), 0, 1)

    def summed(ref):
        all_parts = ref[...].astype(F32)
        total = all_parts[:block]
        for q in range(1, coil_parts):
            total = total + all_parts[q * block : q * block + block]
        return jnp.swapaxes(total, 0, 1)

    coils = maps_in.shape[0]
    for copy in loads[3:]:
        copy.wait()
    row = Row(
        jnp.concatenate([mask] * coils, axis=0),
        (c_ref[...], s_ref[...]), (zc_ref[...], zs_ref[...]),
    )
    weighted = weight_ref[0] * row.mask
    start = []
    for part in planes_of(k_ref[...]):
        measured = row.mask * part
        start.append(measured - weighted * (measured - measured))
    images = row.inverse(*start)
    arrived(0, maps_row)
    row.take_maps(slots_of(maps_row))
    y_src[...] = jnp.stack(row.collect(*images), axis=1).astype(BF)
    to_holders(3, y_src, y_dst)
    arrived(2, cot_row)
    d_src[...] = jnp.stack(row.normal(slots_of(cot_row)), axis=1).astype(BF)
    to_holders(4, d_src, d_dst)

    def exchange_edges(which, src, dst, count):
        def link(side, coil):
            return pltpu.make_async_remote_copy(
                src.at[side], dst.at[1 - side],
                edge_send.at[which * 2 + side], edge_recv.at[which * 2 + 1 - side],
                device_id={"section": me_s, "coil": coil}, device_id_type=pl.DeviceIdType.MESH,
            )

        def coming(side):
            pltpu.make_async_copy(dst.at[side], dst.at[side], edge_recv.at[which * 2 + side]).wait()

        pl.when(me_x > 0)(lambda: link(0, me_c - 1).start())
        pl.when(me_x < columns - 1)(lambda: link(1, me_c + 1).start())
        pl.when(me_x > 0)(lambda: coming(0))
        pl.when(me_x < columns - 1)(lambda: coming(1))

    def open_window(first, planes, which, src, dst):
        for i, plane in enumerate(planes):
            plane = rounded(plane)
            win[first + i, HALO : HALO + block] = plane
            src[0, i] = plane[:HALO].astype(BF)
            src[1, i] = plane[block - HALO :].astype(BF)
        exchange_edges(which, src, dst, len(planes))
        for i in range(len(planes)):
            win[first + i, :HALO] = dst[0, i].astype(F32)
            win[first + i, HALO + block :] = dst[1, i].astype(F32)

    inner = slice(HALO, HALO + block)

    @pl.when(active)
    def _():
        net = Refiner(
            kin_ref, bin_ref, kout_ref, bout_ref, inside, taps_ref, hidden_ref, slope_ref
        )
        arrived(1, gain_all)
        gains = jnp.sum(gain_all[...].astype(F32), axis=0)
        arrived(3, y_dst)
        total = summed(y_dst)
        open_window(0, [total[0], total[1], gains], 0, edge_src, edge_dst)
        gain = win[2]
        m0 = net.refine(0, [rounded(win[0]), rounded(win[1])])
        m_src[...] = jnp.stack([m0[0][inner], m0[1][inner]], axis=1).astype(BF)
        to_owners(5, m_src, m_dst)
        for i in (0, 1):
            state_ref[i] = win[i] + gain * m0[i]
        m1 = net.refine(1, [rounded(state_ref[0]), rounded(state_ref[1])])
        for i in (0, 1):
            state_ref[i] = state_ref[i] + gain * m1[i]
        ubar1 = net.pull_back(1, [rounded(gain * window[i]) for i in (0, 1)])
        for i in (0, 1):
            ubar_ref[i] = ubar1[i]
        arrived(4, d_dst)
        total = summed(d_dst)
        open_window(3, [total[0], total[1]], 1, edge2_src, edge2_dst)
        w0 = weight_ref[0]
        w1 = weight_ref[1]
        mbar0 = [
            rounded(gain * window[i] - w1 * win[3 + i] + gain * ubar_ref[i]) for i in (0, 1)
        ]
        ubar0 = net.pull_back(0, mbar0)
        kept = w0 + (1.0 - w0)
        out = [
            (w1 + kept * (1.0 - w1)) * window[i] + kept * ubar_ref[i] + ubar0[i]
            for i in (0, 1)
        ]
        t_src[...] = jnp.stack([out[0][inner], out[1][inner]], axis=1).astype(BF)
        to_owners(6, t_src, t_dst)

    arrived(5, m_dst)
    e_src[...] = jnp.stack(row.normal(slots_of(m_dst)), axis=1).astype(BF)
    to_holders(7, e_src, e_dst)
    arrived(6, t_dst)
    real, imag = row.expand(slots_of(t_dst))
    grad_ref[...] = packed([row.mask * real, row.mask * imag], half)

    @pl.when(active)
    def _():
        arrived(7, e_dst)
        total = summed(e_dst)
        for i in (0, 1):
            image_src[0, i] = (state_ref[i, inner] - weight_ref[1] * total[i]).astype(BF)

        @pl.loop(0, coil_parts)
        def _(q):
            push(8, image_src.at[0], image_dst.at[me_x], me_s, q)

    arrived(8, image_dst)
    for x in range(columns):
        image_ref[x * block : x * block + block] = packed([image_dst[x, i].astype(F32) for i in (0, 1)], half)

    left(0, maps_ref.at[pl.ds(0, parts - 1)])
    left(2, cot_ref.at[pl.ds(0, parts - 1)])
    if columns > 1:
        whenever(active, lambda: left(1, gain_ref.at[pl.ds(0, columns - 1)]), lambda: left(1, gain_ref))
    else:
        pl.when(jnp.logical_not(active))(lambda: left(1, gain_ref))
    for index, src in ((3, y_src), (4, d_src), (7, e_src)):
        whenever(
            to_self,
            functools.partial(left, index, src.at[pl.ds(0, parts - 1)]),
            functools.partial(left, index, src),
        )

    @pl.when(active)
    def _():
        for index, like in ((5, e_dst), (6, e_dst)):
            whenever(
                to_self,
                functools.partial(left, index, like.at[pl.ds(0, block * coil_parts - 1)]),
                functools.partial(left, index, like),
            )
        left(8, image_src)
        for which, src in ((0, edge_src), (1, edge2_src)):
            for side, there in ((0, me_x > 0), (1, me_x < columns - 1)):
                def gone(which=which, side=side, src=src):
                    pltpu.make_async_copy(
                        src.at[side], src.at[side], edge_send.at[which * 2 + side]
                    ).wait()

                pl.when(there)(gone)


VMEM = pl.BlockSpec(memory_space=pltpu.VMEM)
SMEM = pl.BlockSpec(memory_space=pltpu.SMEM)


def body(kspace, coil_maps, sampling, dc_weight, kernel_in, bias_in, kernel_out, bias_out, cotangent):
    coils, slots, _, width_two = kspace.shape
    rows = coil_maps.shape[2]
    half = width_two // 2
    volumes, depth, _ = sampling.shape
    coil_parts = lax.axis_size("coil")
    parts = lax.axis_size("section")
    columns = coil_parts // 2
    block = rows // columns
    high = block + 2 * HALO

    cosine, sine = line_tables(half)
    zcos, zsin = depth_tables(depth, volumes * coils)
    operands = (
        coil_maps[:, 0], cotangent[0], sampling.reshape(slots, half), kspace.reshape(coils * slots, width_two),
        cosine, sine, zcos, zsin,
    )

    pair = pltpu.VMEM((slots, 2, WIDE), BF)
    gathered = pltpu.VMEM((coil_parts * block, 2, WIDE), BF)
    owned = pltpu.VMEM((block, 2, WIDE), BF)
    plane2 = pltpu.VMEM((2, high, WIDE), F32)
    hidden = pltpu.VMEM((HID, high, WIDE), F32)
    image, grad = pl.pallas_call(
        functools.partial(cascade_kernel, parts, coil_parts),
        out_shape=(
            jax.ShapeDtypeStruct((rows, width_two), F32),
            jax.ShapeDtypeStruct((coils * slots, width_two), F32),
        ),
        in_specs=[SMEM] * 5 + [pl.BlockSpec(memory_space=pl.ANY)] * 8,
        out_specs=(VMEM, VMEM),
        scratch_shapes=[
            *(pltpu.VMEM(x.shape, x.dtype) for x in operands),
            pltpu.SemaphoreType.DMA((8,)),
            pltpu.VMEM((rows, coils, width_two), BF),
            pltpu.VMEM((rows, 2, WIDE), BF),
            pltpu.VMEM((columns, block, WIDE), BF),
            pltpu.VMEM((2, rows + 2 * HALO, WIDE), F32),
            pltpu.VMEM((slots, coils, width_two), BF),
            pair,
            pltpu.VMEM((coil_parts, block, WIDE), BF),
            pair, gathered, pair, gathered, pair, gathered,
            pltpu.VMEM((2, 3, HALO, WIDE), BF), pltpu.VMEM((2, 3, HALO, WIDE), BF),
            pltpu.VMEM((2, 2, HALO, WIDE), BF), pltpu.VMEM((2, 2, HALO, WIDE), BF),
            pltpu.VMEM((5, high, WIDE), F32),
            owned, pair, owned, pair,
            pltpu.VMEM((coil_parts - 1, 2, block, WIDE), BF),
            pltpu.VMEM((columns, 2, block, WIDE), BF),
            plane2, plane2,
            hidden, hidden, pltpu.VMEM((2, HID, high, WIDE), F32),
            pltpu.SemaphoreType.DMA((9,)), pltpu.SemaphoreType.DMA((9,)),
            pltpu.SemaphoreType.DMA((4,)), pltpu.SemaphoreType.DMA((4,)),
        ],
        compiler_params=pltpu.CompilerParams(collective_id=0, has_side_effects=True),
        name="cascade",
    )(
        jnp.swapaxes(kernel_in, 2, 3), bias_in, kernel_out, bias_out, dc_weight, *operands,
    )
    return image[None], grad.reshape(coils, slots, 1, width_two)


def solution(mesh):
    return jax.shard_map(
        body,
        mesh=mesh,
        in_specs=(
            P("coil", None, "section", None),
            P("coil", "section", None, None),
            P(), P(), P(), P(), P(), P(),
            P("section", None, None),
        ),
        out_specs=(P("section", None, None), P("coil", None, "section", None)),
        check_vma=False,
    )
```

```python
import functools
import math

import jax
import jax.numpy as jnp
import numpy as np
from jax import lax
from jax.experimental import pallas as pl
from jax.experimental.pallas import tpu as pltpu
from jax.sharding import PartitionSpec as P

BF = jnp.bfloat16
F32 = jnp.float32
HID = 18
WIDE = 384
HALO = 8


def tables(count, wide):
    index = np.arange(count)
    angle = (index[:, None] * index[None, :] % count) * (2.0 * math.pi / count)
    cosine = np.zeros((wide, wide), np.float32)
    sine = np.zeros((wide, wide), np.float32)
    cosine[:count, :count] = np.cos(angle) / math.sqrt(count)
    sine[:count, :count] = np.sin(angle) / math.sqrt(count)
    return cosine, sine


def line_tables(count):
    cosine, sine = tables(count, WIDE)
    return jnp.asarray(cosine).astype(BF), jnp.asarray(sine).astype(BF)


def depth_tables(depth, blocks):
    cosine, sine = tables(depth, depth)
    eye = np.eye(blocks, dtype=np.float32)
    return jnp.asarray(np.kron(eye, cosine)).astype(BF), jnp.asarray(np.kron(eye, sine)).astype(BF)


def dot(a, b):
    return jnp.dot(a, b, preferred_element_type=F32)


def line_transform(real, imag, cosine, sine, sign):
    rows = real.shape[0]
    both = jnp.concatenate([real, imag], axis=0).astype(BF)
    straight = dot(both, cosine)
    crossed = dot(both, sine)
    return straight[:rows] - sign * crossed[rows:], straight[rows:] + sign * crossed[:rows]


def depth_transform(real, imag, cosine, sine, sign):
    both = jnp.concatenate([real, imag], axis=1).astype(BF)
    straight = dot(cosine, both)
    crossed = dot(sine, both)
    return (
        straight[:, :WIDE] - sign * crossed[:, WIDE:],
        straight[:, WIDE:] + sign * crossed[:, :WIDE],
    )


class Row:
    def __init__(self, mask, line, depth):
        self.mask = mask
        self.line = line
        self.depth = depth

    def take_maps(self, planes):
        self.coils = planes.shape[0]
        stacked = jnp.concatenate([planes[i] for i in range(self.coils)], axis=0)
        self.maps_real, self.maps_imag = planes_of(stacked)

    def expand(self, picture):
        real = jnp.concatenate([picture[0]] * self.coils, axis=0)
        imag = jnp.concatenate([picture[1]] * self.coils, axis=0)
        out = (
            self.maps_real * real - self.maps_imag * imag,
            self.maps_real * imag + self.maps_imag * real,
        )
        out = line_transform(*out, *self.line, -1.0)
        return depth_transform(*out, *self.depth, -1.0)

    def inverse(self, real, imag):
        real, imag = depth_transform(real, imag, *self.depth, 1.0)
        return line_transform(real, imag, *self.line, 1.0)

    def collect(self, real, imag):
        out_real = self.maps_real * real + self.maps_imag * imag
        out_imag = self.maps_real * imag - self.maps_imag * real
        n = out_real.shape[0] // self.coils
        return [
            sum(out[i * n : i * n + n] for i in range(self.coils)) for out in (out_real, out_imag)
        ]

    def normal(self, picture):
        real, imag = self.expand(picture)
        return self.collect(*self.inverse(self.mask * real, self.mask * imag))


def shifted(x, down, right):
    if down:
        x = pltpu.roll(x, (-down) % x.shape[0], 0)
    if right:
        x = pltpu.roll(x, (-right) % x.shape[1], 1)
    return x


def widen(x):
    return jnp.concatenate([x, jnp.zeros((x.shape[0], WIDE - x.shape[1]), x.dtype)], axis=1)


def planes_of(x):
    half = x.shape[1] // 2
    return [widen(x[:, :half].astype(F32)), widen(x[:, half:].astype(F32))]


def packed(planes, half):
    return jnp.concatenate([planes[0][:, :half], planes[1][:, :half]], axis=1)


def rounded(x):
    return x.astype(BF).astype(F32)


class Refiner:
    def __init__(self, kin_ref, bin_ref, kout_ref, bout_ref, inside, taps_ref, hidden_ref, slope_ref):
        self.kin, self.bin, self.kout, self.bout = kin_ref, bin_ref, kout_ref, bout_ref
        self.inside = inside
        self.taps, self.hidden, self.slope = taps_ref, hidden_ref, slope_ref

    def spread_taps(self, planes, sign):
        for channel in (0, 1):
            for b in range(3):
                moved = shifted(planes[channel], 0, sign * (b - 1))
                for a in range(3):
                    self.taps[(a * 3 + b) * 2 + channel] = shifted(moved, sign * (a - 1), 0)

    def gather_taps(self, sign):
        planes = []
        for channel in (0, 1):
            plane = None
            for b in range(3):
                column = None
                for a in range(3):
                    piece = shifted(self.taps[(a * 3 + b) * 2 + channel], sign * (a - 1), 0)
                    column = piece if column is None else column + piece
                column = shifted(column, 0, sign * (b - 1))
                plane = column if plane is None else plane + column
            planes.append(plane)
        return planes

    @staticmethod
    def mix(source_ref, weight_of, first):
        total = first
        for k in range(HID):
            term = weight_of(k) * source_ref[k]
            total = term if total is None else total + term
        return total

    def into_hidden(self, t, o, k):
        return self.kin[t, k // 2, k % 2, o]

    def out_of_hidden(self, t, k, o):
        if isinstance(k, int):
            return self.kout[t, k // 2, k % 2, o]
        return self.kout[t, lax.div(k, 2), lax.rem(k, 2), o]

    def refine(self, t, planes):
        self.spread_taps(planes, 1)

        @pl.loop(0, HID)
        def _(o):
            first = jnp.full(self.inside.shape, self.bin[t, o], F32)
            pre = self.mix(self.taps, lambda k: self.into_hidden(t, o, k), first)
            gate = jax.nn.sigmoid(pre)
            self.hidden[o] = self.inside * pre * gate
            self.slope[t, o] = self.inside * gate * (1.0 + pre * (1.0 - gate))

        @pl.loop(0, HID)
        def _(k):
            self.taps[k] = self.mix(self.hidden, lambda o: self.out_of_hidden(t, k, o), None)

        planes = self.gather_taps(1)
        return [rounded(planes[i] + self.bout[t, i]) for i in (0, 1)]

    def pull_back(self, t, planes):
        self.spread_taps(planes, -1)

        @pl.loop(0, HID)
        def _(o):
            self.hidden[o] = self.slope[t, o] * self.mix(
                self.taps, lambda k: self.out_of_hidden(t, k, o), None
            )

        @pl.loop(0, HID)
        def _(k):
            tap = lax.div(k, 2)
            channel = lax.rem(k, 2)
            self.taps[k] = self.mix(self.hidden, lambda o: self.kin[t, tap, channel, o], None)

        return [rounded(x) for x in self.gather_taps(-1)]


def clear(first_ref, second_ref, side):
    first_ref[side] = jnp.zeros(first_ref.shape[1:], first_ref.dtype)
    second_ref[side] = jnp.zeros(second_ref.shape[1:], second_ref.dtype)


def cascade_kernel(
    parts, coil_parts,
    kin_ref, bin_ref, kout_ref, bout_ref, weight_ref,
    maps_any, cot_any, sampling_any, k_any, c_any, s_any, zc_any, zs_any,
    image_ref, grad_ref,
    maps_in, cot_in, sampling_in, k_ref, c_ref, s_ref, zc_ref, zs_ref, load,
    maps_ref, cot_ref, gain_ref, cot_pad,
    maps_row, cot_row, gain_all,
    y_src, y_dst, d_src, d_dst, e_src, e_dst,
    edge_src, edge_dst, edge2_src, edge2_dst, win,
    m_src, m_dst, t_src, t_dst, image_src, image_dst, twin_src, twin_dst, state_ref, ubar_ref,
    taps_ref, hidden_ref, slope_ref,
    send, recv, edge_send, edge_recv,
):
    rows = maps_ref.shape[0]
    half = sampling_in.shape[1]
    columns = coil_parts // 2
    block = rows // columns
    me_s = lax.axis_index("section")
    me_c = lax.axis_index("coil")
    me_x = lax.rem(me_c, columns)
    me_hi = lax.div(me_c, columns)
    my_block = lax.div(me_s, block)
    active = me_hi == lax.rem(me_s, 2)
    to_self = jnp.logical_and(active, me_x == my_block)

    def holder(slot, x):
        return lax.rem(slot, 2) * columns + x

    def whenever(condition, yes, no=None):
        pl.when(condition)(yes)
        if no is not None:
            pl.when(jnp.logical_not(condition))(no)

    def near(index, src, dst):
        pltpu.make_async_copy(src, dst, recv.at[index]).start()

    def far(index, src, dst, section, coil):
        pltpu.make_async_remote_copy(
            src, dst, send.at[index], recv.at[index],
            device_id={"section": section, "coil": coil}, device_id_type=pl.DeviceIdType.MESH,
        ).start()

    def push(index, src, dst, section, coil):
        mine = jnp.logical_and(section == me_s, coil == me_c)
        whenever(
            mine,
            lambda: near(index, src, dst),
            lambda: far(index, src, dst, section, coil),
        )

    def arrived(index, ref):
        pltpu.make_async_copy(ref, ref, recv.at[index]).wait()

    def left(index, ref):
        pltpu.make_async_copy(ref, ref, send.at[index]).wait()

    barrier = pltpu.get_barrier_semaphore()

    def greet(section, coil):
        pl.semaphore_signal(
            barrier, 1, device_id={"section": section, "coil": coil}, device_id_type=pl.DeviceIdType.MESH
        )

    @pl.loop(1, parts)
    def _(k):
        greet(lax.rem(me_s + k, parts), me_c)

    @pl.loop(1, coil_parts)
    def _(k):
        greet(me_s, lax.rem(me_c + k, coil_parts))

    loads = [
        pltpu.make_async_copy(src, dst, load.at[i])
        for i, (src, dst) in enumerate(
            zip(
                (maps_any, cot_any, sampling_any, k_any, c_any, s_any, zc_any, zs_any),
                (maps_in, cot_in, sampling_in, k_ref, c_ref, s_ref, zc_ref, zs_ref),
            )
        )
    ]
    for copy in loads:
        copy.start()

    loads[0].wait()
    maps_ref[...] = jnp.swapaxes(maps_in[...], 0, 1)
    gain = None
    for i in range(maps_in.shape[0]):
        for plane in planes_of(maps_in[i]):
            gain = plane * plane if gain is None else gain + plane * plane
    for x in range(columns):
        gain_ref[x] = gain[x * block : x * block + block].astype(BF)
    loads[1].wait()
    cot_planes = planes_of(cot_in[...])
    cot_ref[...] = jnp.stack(cot_planes, axis=1).astype(BF)
    for i in (0, 1):
        cot_pad[i, :HALO] = jnp.zeros((HALO, WIDE), F32)
        cot_pad[i, HALO + rows :] = jnp.zeros((HALO, WIDE), F32)
        cot_pad[i, HALO : HALO + rows] = cot_planes[i]
    high = block + 2 * HALO
    first_row = pl.multiple_of(me_x * block, HALO)
    window = [cot_pad[i, pl.ds(first_row, high), :] for i in (0, 1)]
    place = first_row - HALO + lax.broadcasted_iota(jnp.int32, (high, WIDE), 0)
    line = lax.broadcasted_iota(jnp.int32, (high, WIDE), 1)
    inside = jnp.where((place >= 0) & (place < rows) & (line < half), 1.0, 0.0).astype(F32)
    loads[2].wait()
    mask = widen(sampling_in[...].astype(F32))

    pl.semaphore_wait(barrier, parts - 1 + coil_parts - 1)

    def to_section(index, src, dst):
        near(index, src.at[me_s], dst.at[me_s])

        @pl.loop(1, parts)
        def _(k):
            p = lax.rem(me_s + k, parts)
            far(index, src.at[p], dst.at[me_s], p, me_c)

    to_section(0, maps_ref, maps_row)

    @pl.loop(0, columns)
    def _(x):
        push(1, gain_ref.at[x], gain_all.at[me_c], me_s, holder(me_s, x))

    pl.when(me_x == 0)(lambda: clear(edge_dst, edge2_dst, 0))
    pl.when(me_x == columns - 1)(lambda: clear(edge_dst, edge2_dst, 1))

    spot = me_c * block + lax.rem(me_s, block)

    def to_holders(index, src, dst):
        push(index, src.at[me_s], dst.at[spot], me_s, holder(me_s, my_block))

        @pl.loop(1, parts)
        def _(k):
            p = lax.rem(me_s + k, parts)
            far(index, src.at[p], dst.at[spot], p, holder(p, my_block))

    def to_both_holders(index, src, dst):
        for hi in (0, 1):
            push(index, src.at[me_s], dst.at[spot], me_s, hi * columns + my_block)

        @pl.loop(1, parts)
        def _(k):
            p = lax.rem(me_s + k, parts)
            for hi in (0, 1):
                far(index, src.at[p], dst.at[spot], p, hi * columns + my_block)

    def to_owners(index, src, dst):
        @pl.loop(0, block)
        def _(i):
            push(index, src.at[i], dst.at[me_s], me_x * block + i, me_c)

            @pl.loop(1, coil_parts)
            def _(k):
                far(index, src.at[i], dst.at[me_s], me_x * block + i, lax.rem(me_c + k, coil_parts))

    def slots_of(ref):
        return jnp.swapaxes(ref[...].astype(F32), 0, 1)

    def summed(ref):
        all_parts = ref[...].astype(F32)
        total = all_parts[:block]
        for q in range(1, coil_parts):
            total = total + all_parts[q * block : q * block + block]
        return jnp.swapaxes(total, 0, 1)

    coils = maps_in.shape[0]
    for copy in loads[3:]:
        copy.wait()
    row = Row(
        jnp.concatenate([mask] * coils, axis=0),
        (c_ref[...], s_ref[...]), (zc_ref[...], zs_ref[...]),
    )
    weighted = weight_ref[0] * row.mask
    start = []
    for part in planes_of(k_ref[...]):
        measured = row.mask * part
        start.append(measured - weighted * (measured - measured))
    images = row.inverse(*start)
    arrived(0, maps_row)
    row.take_maps(slots_of(maps_row))
    y_src[...] = jnp.stack(row.collect(*images), axis=1).astype(BF)
    to_holders(3, y_src, y_dst)
    to_section(2, cot_ref, cot_row)

    def exchange_edges(which, src, dst, count):
        def link(side, coil):
            return pltpu.make_async_remote_copy(
                src.at[side], dst.at[1 - side],
                edge_send.at[which * 2 + side], edge_recv.at[which * 2 + 1 - side],
                device_id={"section": me_s, "coil": coil}, device_id_type=pl.DeviceIdType.MESH,
            )

        def coming(side):
            pltpu.make_async_copy(dst.at[side], dst.at[side], edge_recv.at[which * 2 + side]).wait()

        pl.when(me_x > 0)(lambda: link(0, me_c - 1).start())
        pl.when(me_x < columns - 1)(lambda: link(1, me_c + 1).start())
        pl.when(me_x > 0)(lambda: coming(0))
        pl.when(me_x < columns - 1)(lambda: coming(1))

    def open_window(first, planes, which, src, dst):
        for i, plane in enumerate(planes):
            plane = rounded(plane)
            win[first + i, HALO : HALO + block] = plane
            src[0, i] = plane[:HALO].astype(BF)
            src[1, i] = plane[block - HALO :].astype(BF)
        exchange_edges(which, src, dst, len(planes))
        for i in range(len(planes)):
            win[first + i, :HALO] = dst[0, i].astype(F32)
            win[first + i, HALO + block :] = dst[1, i].astype(F32)

    inner = slice(HALO, HALO + block)

    net = Refiner(kin_ref, bin_ref, kout_ref, bout_ref, inside, taps_ref, hidden_ref, slope_ref)

    @pl.when(active)
    def _():
        arrived(1, gain_all)
        gains = jnp.sum(gain_all[...].astype(F32), axis=0)
        arrived(3, y_dst)
        total = summed(y_dst)
        open_window(0, [total[0], total[1], gains], 0, edge_src, edge_dst)
        m0 = net.refine(0, [rounded(win[0]), rounded(win[1])])
        m_src[...] = jnp.stack([m0[0][inner], m0[1][inner]], axis=1).astype(BF)
        to_owners(5, m_src, m_dst)
        for i in (0, 1):
            state_ref[i] = win[i] + win[2] * m0[i]

    arrived(2, cot_row)
    d_src[...] = jnp.stack(row.normal(slots_of(cot_row)), axis=1).astype(BF)
    to_holders(4, d_src, d_dst)

    twin = (1 - me_hi) * columns + me_x

    @pl.when(active)
    def _():
        gain = win[2]
        m1 = net.refine(1, [rounded(state_ref[0]), rounded(state_ref[1])])
        for i in (0, 1):
            twin_src[i] = (state_ref[i] + gain * m1[i])[inner]
        far(9, twin_src, twin_dst, me_s, twin)
        ubar1 = net.pull_back(1, [rounded(gain * window[i]) for i in (0, 1)])
        for i in (0, 1):
            ubar_ref[i] = ubar1[i]

    arrived(5, m_dst)
    e_src[...] = jnp.stack(row.normal(slots_of(m_dst)), axis=1).astype(BF)
    to_both_holders(7, e_src, e_dst)

    @pl.when(active)
    def _():
        gain = win[2]
        arrived(4, d_dst)
        total = summed(d_dst)
        open_window(3, [total[0], total[1]], 1, edge2_src, edge2_dst)
        w0 = weight_ref[0]
        w1 = weight_ref[1]
        mbar0 = [
            rounded(gain * window[i] - w1 * win[3 + i] + gain * ubar_ref[i]) for i in (0, 1)
        ]
        ubar0 = net.pull_back(0, mbar0)
        kept = w0 + (1.0 - w0)
        out = [
            (w1 + kept * (1.0 - w1)) * window[i] + kept * ubar_ref[i] + ubar0[i] for i in (0, 1)
        ]
        t_src[...] = jnp.stack([out[0][inner], out[1][inner]], axis=1).astype(BF)
        to_owners(6, t_src, t_dst)

    def image_block(base_ref):
        total = summed(e_dst)
        for i in (0, 1):
            image_src[0, i] = (base_ref[i] - weight_ref[1] * total[i]).astype(BF)

    arrived(7, e_dst)
    pl.when(jnp.logical_not(active))(lambda: arrived(9, twin_dst))
    whenever(active, lambda: image_block(twin_src), lambda: image_block(twin_dst))

    @pl.loop(0, columns)
    def _(x):
        push(8, image_src.at[0], image_dst.at[me_x], me_s, me_hi * columns + x)

    arrived(6, t_dst)
    real, imag = row.expand(slots_of(t_dst))
    grad_ref[...] = packed([row.mask * real, row.mask * imag], half)
    arrived(8, image_dst)
    for x in range(columns):
        image_ref[x * block : x * block + block] = packed([image_dst[x, i].astype(F32) for i in (0, 1)], half)

    left(0, maps_ref.at[pl.ds(0, parts - 1)])
    left(2, cot_ref.at[pl.ds(0, parts - 1)])
    if columns > 1:
        whenever(active, lambda: left(1, gain_ref.at[pl.ds(0, columns - 1)]), lambda: left(1, gain_ref))
    else:
        pl.when(jnp.logical_not(active))(lambda: left(1, gain_ref))
    for index, src in ((3, y_src), (4, d_src)):
        whenever(
            to_self,
            functools.partial(left, index, src.at[pl.ds(0, parts - 1)]),
            functools.partial(left, index, src),
        )

    whenever(
        me_x == my_block,
        functools.partial(left, 7, e_dst.at[pl.ds(0, 2 * parts - 1)]),
        functools.partial(left, 7, e_dst),
    )
    if columns > 1:
        left(8, image_src)

    @pl.when(active)
    def _():
        for index, like in ((5, e_dst), (6, e_dst)):
            whenever(
                to_self,
                functools.partial(left, index, like.at[pl.ds(0, block * coil_parts - 1)]),
                functools.partial(left, index, like),
            )
        left(9, twin_src)
        for which, src in ((0, edge_src), (1, edge2_src)):
            for side, there in ((0, me_x > 0), (1, me_x < columns - 1)):
                def gone(which=which, side=side, src=src):
                    pltpu.make_async_copy(
                        src.at[side], src.at[side], edge_send.at[which * 2 + side]
                    ).wait()

                pl.when(there)(gone)


VMEM = pl.BlockSpec(memory_space=pltpu.VMEM)
SMEM = pl.BlockSpec(memory_space=pltpu.SMEM)


def body(kspace, coil_maps, sampling, dc_weight, kernel_in, bias_in, kernel_out, bias_out, cotangent):
    coils, slots, _, width_two = kspace.shape
    rows = coil_maps.shape[2]
    half = width_two // 2
    volumes, depth, _ = sampling.shape
    coil_parts = lax.axis_size("coil")
    parts = lax.axis_size("section")
    columns = coil_parts // 2
    block = rows // columns
    high = block + 2 * HALO

    cosine, sine = line_tables(half)
    zcos, zsin = depth_tables(depth, volumes * coils)
    operands = (
        coil_maps[:, 0], cotangent[0], sampling.reshape(slots, half), kspace.reshape(coils * slots, width_two),
        cosine, sine, zcos, zsin,
    )

    pair = pltpu.VMEM((slots, 2, WIDE), BF)
    gathered = pltpu.VMEM((coil_parts * block, 2, WIDE), BF)
    owned = pltpu.VMEM((block, 2, WIDE), BF)
    plane2 = pltpu.VMEM((2, high, WIDE), F32)
    hidden = pltpu.VMEM((HID, high, WIDE), F32)
    image, grad = pl.pallas_call(
        functools.partial(cascade_kernel, parts, coil_parts),
        out_shape=(
            jax.ShapeDtypeStruct((rows, width_two), F32),
            jax.ShapeDtypeStruct((coils * slots, width_two), F32),
        ),
        in_specs=[SMEM] * 5 + [pl.BlockSpec(memory_space=pl.ANY)] * 8,
        out_specs=(VMEM, VMEM),
        scratch_shapes=[
            *(pltpu.VMEM(x.shape, x.dtype) for x in operands),
            pltpu.SemaphoreType.DMA((8,)),
            pltpu.VMEM((rows, coils, width_two), BF),
            pltpu.VMEM((rows, 2, WIDE), BF),
            pltpu.VMEM((columns, block, WIDE), BF),
            pltpu.VMEM((2, rows + 2 * HALO, WIDE), F32),
            pltpu.VMEM((slots, coils, width_two), BF),
            pair,
            pltpu.VMEM((coil_parts, block, WIDE), BF),
            pair, gathered, pair, gathered, pair, gathered,
            pltpu.VMEM((2, 3, HALO, WIDE), BF), pltpu.VMEM((2, 3, HALO, WIDE), BF),
            pltpu.VMEM((2, 2, HALO, WIDE), BF), pltpu.VMEM((2, 2, HALO, WIDE), BF),
            pltpu.VMEM((5, high, WIDE), F32),
            owned, pair, owned, pair,
            pltpu.VMEM((max(columns - 1, 1), 2, block, WIDE), BF),
            pltpu.VMEM((columns, 2, block, WIDE), BF),
            pltpu.VMEM((2, block, WIDE), F32), pltpu.VMEM((2, block, WIDE), F32),
            plane2, plane2,
            hidden, hidden, pltpu.VMEM((2, HID, high, WIDE), F32),
            pltpu.SemaphoreType.DMA((10,)), pltpu.SemaphoreType.DMA((10,)),
            pltpu.SemaphoreType.DMA((4,)), pltpu.SemaphoreType.DMA((4,)),
        ],
        compiler_params=pltpu.CompilerParams(collective_id=0, has_side_effects=True),
        name="cascade",
    )(
        jnp.swapaxes(kernel_in, 2, 3), bias_in, kernel_out, bias_out, dc_weight, *operands,
    )
    return image[None], grad.reshape(coils, slots, 1, width_two)


def solution(mesh):
    return jax.shard_map(
        body,
        mesh=mesh,
        in_specs=(
            P("coil", None, "section", None),
            P("coil", "section", None, None),
            P(), P(), P(), P(), P(), P(),
            P("section", None, None),
        ),
        out_specs=(P("section", None, None), P("coil", None, "section", None)),
        check_vma=False,
    )
```

```python
import functools
import math

import jax
import jax.numpy as jnp
import numpy as np
from jax import lax
from jax.experimental import pallas as pl
from jax.experimental.pallas import tpu as pltpu
from jax.sharding import PartitionSpec as P

BF = jnp.bfloat16
F32 = jnp.float32
HID = 18
WIDE = 384
HALO = 8


def tables(count, wide):
    index = np.arange(count)
    angle = (index[:, None] * index[None, :] % count) * (2.0 * math.pi / count)
    cosine = np.zeros((wide, wide), np.float32)
    sine = np.zeros((wide, wide), np.float32)
    cosine[:count, :count] = np.cos(angle) / math.sqrt(count)
    sine[:count, :count] = np.sin(angle) / math.sqrt(count)
    return cosine, sine


def line_tables(count):
    cosine, sine = tables(count, WIDE)
    return jnp.asarray(cosine).astype(BF), jnp.asarray(sine).astype(BF)


def depth_tables(depth, blocks):
    cosine, sine = tables(depth, depth)
    eye = np.eye(blocks, dtype=np.float32)
    return jnp.asarray(np.kron(eye, cosine)).astype(BF), jnp.asarray(np.kron(eye, sine)).astype(BF)


def dot(a, b):
    return jnp.dot(a, b, preferred_element_type=F32)


def line_transform(real, imag, cosine, sine, sign):
    rows = real.shape[0]
    both = jnp.concatenate([real, imag], axis=0).astype(BF)
    straight = dot(both, cosine)
    crossed = dot(both, sine)
    return straight[:rows] - sign * crossed[rows:], straight[rows:] + sign * crossed[:rows]


def depth_transform(real, imag, cosine, sine, sign):
    both = jnp.concatenate([real, imag], axis=1).astype(BF)
    straight = dot(cosine, both)
    crossed = dot(sine, both)
    return (
        straight[:, :WIDE] - sign * crossed[:, WIDE:],
        straight[:, WIDE:] + sign * crossed[:, :WIDE],
    )


class Row:
    def __init__(self, mask, line, depth):
        self.mask = mask
        self.line = line
        self.depth = depth

    def take_maps(self, planes):
        self.coils = planes.shape[0]
        stacked = jnp.concatenate([planes[i] for i in range(self.coils)], axis=0)
        self.maps_real, self.maps_imag = planes_of(stacked)

    def expand(self, picture):
        real = jnp.concatenate([picture[0]] * self.coils, axis=0)
        imag = jnp.concatenate([picture[1]] * self.coils, axis=0)
        out = (
            self.maps_real * real - self.maps_imag * imag,
            self.maps_real * imag + self.maps_imag * real,
        )
        out = line_transform(*out, *self.line, -1.0)
        return depth_transform(*out, *self.depth, -1.0)

    def inverse(self, real, imag):
        real, imag = depth_transform(real, imag, *self.depth, 1.0)
        return line_transform(real, imag, *self.line, 1.0)

    def collect(self, real, imag):
        out_real = self.maps_real * real + self.maps_imag * imag
        out_imag = self.maps_real * imag - self.maps_imag * real
        n = out_real.shape[0] // self.coils
        return [
            sum(out[i * n : i * n + n] for i in range(self.coils)) for out in (out_real, out_imag)
        ]

    def normal(self, picture):
        real, imag = self.expand(picture)
        return self.collect(*self.inverse(self.mask * real, self.mask * imag))


def shifted(x, down, right):
    if down:
        x = pltpu.roll(x, (-down) % x.shape[0], 0)
    if right:
        x = pltpu.roll(x, (-right) % x.shape[1], 1)
    return x


def widen(x):
    return jnp.concatenate([x, jnp.zeros((x.shape[0], WIDE - x.shape[1]), x.dtype)], axis=1)


def planes_of(x):
    half = x.shape[1] // 2
    return [widen(x[:, :half].astype(F32)), widen(x[:, half:].astype(F32))]


def packed(planes, half):
    return jnp.concatenate([planes[0][:, :half], planes[1][:, :half]], axis=1)


def rounded(x):
    return x.astype(BF).astype(F32)


class Refiner:
    def __init__(self, kin_ref, bin_ref, kout_ref, bout_ref, inside, taps_ref, hidden_ref, slope_ref):
        self.kin, self.bin, self.kout, self.bout = kin_ref, bin_ref, kout_ref, bout_ref
        self.inside = inside
        self.taps, self.hidden, self.slope = taps_ref, hidden_ref, slope_ref

    def spread_taps(self, planes, sign):
        for channel in (0, 1):
            for b in range(3):
                moved = shifted(planes[channel], 0, sign * (b - 1))
                for a in range(3):
                    self.taps[(a * 3 + b) * 2 + channel] = shifted(moved, sign * (a - 1), 0)

    def gather_taps(self, sign):
        planes = []
        for channel in (0, 1):
            plane = None
            for b in range(3):
                column = None
                for a in range(3):
                    piece = shifted(self.taps[(a * 3 + b) * 2 + channel], sign * (a - 1), 0)
                    column = piece if column is None else column + piece
                column = shifted(column, 0, sign * (b - 1))
                plane = column if plane is None else plane + column
            planes.append(plane)
        return planes

    @staticmethod
    def mix(source_ref, weight_of, first):
        total = first
        for k in range(HID):
            term = weight_of(k) * source_ref[k]
            total = term if total is None else total + term
        return total

    def into_hidden(self, t, o, k):
        return self.kin[t, k // 2, k % 2, o]

    def out_of_hidden(self, t, k, o):
        if isinstance(k, int):
            return self.kout[t, k // 2, k % 2, o]
        return self.kout[t, lax.div(k, 2), lax.rem(k, 2), o]

    def refine(self, t, planes):
        self.spread_taps(planes, 1)

        @pl.loop(0, HID)
        def _(o):
            first = jnp.full(self.inside.shape, self.bin[t, o], F32)
            pre = self.mix(self.taps, lambda k: self.into_hidden(t, o, k), first)
            gate = jax.nn.sigmoid(pre)
            self.hidden[o] = self.inside * pre * gate
            self.slope[t, o] = self.inside * gate * (1.0 + pre * (1.0 - gate))

        @pl.loop(0, HID)
        def _(k):
            self.taps[k] = self.mix(self.hidden, lambda o: self.out_of_hidden(t, k, o), None)

        planes = self.gather_taps(1)
        return [rounded(planes[i] + self.bout[t, i]) for i in (0, 1)]

    def pull_back(self, t, planes):
        self.spread_taps(planes, -1)

        @pl.loop(0, HID)
        def _(o):
            self.hidden[o] = self.slope[t, o] * self.mix(
                self.taps, lambda k: self.out_of_hidden(t, k, o), None
            )

        @pl.loop(0, HID)
        def _(k):
            tap = lax.div(k, 2)
            channel = lax.rem(k, 2)
            self.taps[k] = self.mix(self.hidden, lambda o: self.kin[t, tap, channel, o], None)

        return [rounded(x) for x in self.gather_taps(-1)]


def clear(first_ref, second_ref, side):
    first_ref[side] = jnp.zeros(first_ref.shape[1:], first_ref.dtype)
    second_ref[side] = jnp.zeros(second_ref.shape[1:], second_ref.dtype)


def cascade_kernel(
    parts, coil_parts,
    kin_ref, bin_ref, kout_ref, bout_ref, weight_ref,
    maps_any, cot_any, sampling_any, k_any, c_any, s_any, zc_any, zs_any,
    image_ref, grad_ref,
    maps_in, cot_in, sampling_in, k_ref, c_ref, s_ref, zc_ref, zs_ref, load,
    maps_ref, cot_ref, gain_ref, cot_pad,
    maps_row, cot_row, gain_all,
    y_src, y_dst, d_src, d_dst, e_src, share_dst, share_src, e_dst,
    edge_src, edge_dst, edge2_src, edge2_dst, win,
    m_src, m_dst, t_src, t_dst, image_src, image_dst, twin_src, twin_dst, state_ref, ubar_ref,
    taps_ref, hidden_ref, slope_ref,
    send, recv, edge_send, edge_recv,
):
    rows = maps_ref.shape[0]
    half = sampling_in.shape[1]
    columns = coil_parts // 2
    block = rows // columns
    me_s = lax.axis_index("section")
    me_c = lax.axis_index("coil")
    me_x = lax.rem(me_c, columns)
    me_hi = lax.div(me_c, columns)
    my_block = lax.div(me_s, block)
    active = me_hi == lax.rem(me_s, 2)
    to_self = jnp.logical_and(active, me_x == my_block)

    def holder(slot, x):
        return lax.rem(slot, 2) * columns + x

    def whenever(condition, yes, no=None):
        pl.when(condition)(yes)
        if no is not None:
            pl.when(jnp.logical_not(condition))(no)

    def near(index, src, dst):
        pltpu.make_async_copy(src, dst, recv.at[index]).start()

    def far(index, src, dst, section, coil):
        pltpu.make_async_remote_copy(
            src, dst, send.at[index], recv.at[index],
            device_id={"section": section, "coil": coil}, device_id_type=pl.DeviceIdType.MESH,
        ).start()

    def push(index, src, dst, section, coil):
        mine = jnp.logical_and(section == me_s, coil == me_c)
        whenever(
            mine,
            lambda: near(index, src, dst),
            lambda: far(index, src, dst, section, coil),
        )

    def arrived(index, ref):
        pltpu.make_async_copy(ref, ref, recv.at[index]).wait()

    def left(index, ref):
        pltpu.make_async_copy(ref, ref, send.at[index]).wait()

    barrier = pltpu.get_barrier_semaphore()

    def greet(section, coil):
        pl.semaphore_signal(
            barrier, 1, device_id={"section": section, "coil": coil}, device_id_type=pl.DeviceIdType.MESH
        )

    @pl.loop(1, parts)
    def _(k):
        greet(lax.rem(me_s + k, parts), me_c)

    @pl.loop(1, coil_parts)
    def _(k):
        greet(me_s, lax.rem(me_c + k, coil_parts))

    loads = [
        pltpu.make_async_copy(src, dst, load.at[i])
        for i, (src, dst) in enumerate(
            zip(
                (maps_any, cot_any, sampling_any, k_any, c_any, s_any, zc_any, zs_any),
                (maps_in, cot_in, sampling_in, k_ref, c_ref, s_ref, zc_ref, zs_ref),
            )
        )
    ]
    for copy in loads:
        copy.start()

    loads[0].wait()
    maps_ref[...] = jnp.swapaxes(maps_in[...], 0, 1)
    gain = None
    for i in range(maps_in.shape[0]):
        for plane in planes_of(maps_in[i]):
            gain = plane * plane if gain is None else gain + plane * plane
    for x in range(columns):
        gain_ref[x] = gain[x * block : x * block + block].astype(BF)
    loads[1].wait()
    cot_planes = planes_of(cot_in[...])
    cot_ref[...] = jnp.stack(cot_planes, axis=1).astype(BF)
    for i in (0, 1):
        cot_pad[i, :HALO] = jnp.zeros((HALO, WIDE), F32)
        cot_pad[i, HALO + rows :] = jnp.zeros((HALO, WIDE), F32)
        cot_pad[i, HALO : HALO + rows] = cot_planes[i]
    high = block + 2 * HALO
    first_row = pl.multiple_of(me_x * block, HALO)
    window = [cot_pad[i, pl.ds(first_row, high), :] for i in (0, 1)]
    place = first_row - HALO + lax.broadcasted_iota(jnp.int32, (high, WIDE), 0)
    line = lax.broadcasted_iota(jnp.int32, (high, WIDE), 1)
    inside = jnp.where((place >= 0) & (place < rows) & (line < half), 1.0, 0.0).astype(F32)
    loads[2].wait()
    mask = widen(sampling_in[...].astype(F32))

    pl.semaphore_wait(barrier, parts - 1 + coil_parts - 1)

    def to_section(index, src, dst):
        near(index, src.at[me_s], dst.at[me_s])

        @pl.loop(1, parts)
        def _(k):
            p = lax.rem(me_s + k, parts)
            far(index, src.at[p], dst.at[me_s], p, me_c)

    to_section(0, maps_ref, maps_row)

    @pl.loop(0, columns)
    def _(x):
        push(1, gain_ref.at[x], gain_all.at[me_c], me_s, holder(me_s, x))

    pl.when(me_x == 0)(lambda: clear(edge_dst, edge2_dst, 0))
    pl.when(me_x == columns - 1)(lambda: clear(edge_dst, edge2_dst, 1))

    spot = me_c * block + lax.rem(me_s, block)

    def to_holders(index, src, dst):
        push(index, src.at[me_s], dst.at[spot], me_s, holder(me_s, my_block))

        @pl.loop(1, parts)
        def _(k):
            p = lax.rem(me_s + k, parts)
            far(index, src.at[p], dst.at[spot], p, holder(p, my_block))

    def to_owners(index, src, dst):
        @pl.loop(0, block)
        def _(i):
            push(index, src.at[i], dst.at[me_s], me_x * block + i, me_c)

            @pl.loop(1, coil_parts)
            def _(k):
                far(index, src.at[i], dst.at[me_s], me_x * block + i, lax.rem(me_c + k, coil_parts))

    def slots_of(ref):
        return jnp.swapaxes(ref[...].astype(F32), 0, 1)

    def summed(ref):
        all_parts = ref[...].astype(F32)
        total = all_parts[:block]
        for q in range(1, coil_parts):
            total = total + all_parts[q * block : q * block + block]
        return jnp.swapaxes(total, 0, 1)

    coils = maps_in.shape[0]
    for copy in loads[3:]:
        copy.wait()
    row = Row(
        jnp.concatenate([mask] * coils, axis=0),
        (c_ref[...], s_ref[...]), (zc_ref[...], zs_ref[...]),
    )
    weighted = weight_ref[0] * row.mask
    start = []
    for part in planes_of(k_ref[...]):
        measured = row.mask * part
        start.append(measured - weighted * (measured - measured))
    images = row.inverse(*start)
    to_section(2, cot_ref, cot_row)
    arrived(0, maps_row)
    row.take_maps(slots_of(maps_row))
    y_src[...] = jnp.stack(row.collect(*images), axis=1).astype(BF)
    to_holders(3, y_src, y_dst)
    arrived(2, cot_row)
    d_src[...] = jnp.stack(row.normal(slots_of(cot_row)), axis=1).astype(BF)
    to_holders(4, d_src, d_dst)

    def exchange_edges(which, src, dst):
        def link(side, coil):
            return pltpu.make_async_remote_copy(
                src.at[side], dst.at[1 - side],
                edge_send.at[which * 2 + side], edge_recv.at[which * 2 + 1 - side],
                device_id={"section": me_s, "coil": coil}, device_id_type=pl.DeviceIdType.MESH,
            )

        pl.when(me_x > 0)(lambda: link(0, me_c - 1).start())
        pl.when(me_x < columns - 1)(lambda: link(1, me_c + 1).start())

    def open_window(first, planes, which, src, dst):
        for i, plane in enumerate(planes):
            plane = rounded(plane)
            win[first + i, HALO : HALO + block] = plane
            src[0, i] = plane[:HALO].astype(BF)
            src[1, i] = plane[block - HALO :].astype(BF)
        exchange_edges(which, src, dst)

    def close_window(first, count, which, dst):
        def coming(side):
            pltpu.make_async_copy(dst.at[side], dst.at[side], edge_recv.at[which * 2 + side]).wait()

        pl.when(me_x > 0)(lambda: coming(0))
        pl.when(me_x < columns - 1)(lambda: coming(1))
        for i in range(count):
            win[first + i, :HALO] = dst[0, i].astype(F32)
            win[first + i, HALO + block :] = dst[1, i].astype(F32)

    inner = slice(HALO, HALO + block)

    net = Refiner(kin_ref, bin_ref, kout_ref, bout_ref, inside, taps_ref, hidden_ref, slope_ref)

    @pl.when(active)
    def _():
        arrived(1, gain_all)
        gains = jnp.sum(gain_all[...].astype(F32), axis=0)
        arrived(3, y_dst)
        total = summed(y_dst)
        open_window(0, [total[0], total[1], gains], 0, edge_src, edge_dst)
        close_window(0, 3, 0, edge_dst)
        m0 = net.refine(0, [rounded(win[0]), rounded(win[1])])
        m_src[...] = jnp.stack([m0[0][inner], m0[1][inner]], axis=1).astype(BF)
        to_owners(5, m_src, m_dst)
        for i in (0, 1):
            state_ref[i] = win[i] + win[2] * m0[i]
        gain = win[2]
        m1 = net.refine(1, [rounded(state_ref[0]), rounded(state_ref[1])])
        for i in (0, 1):
            twin_src[i] = (state_ref[i] + gain * m1[i])[inner]
        far(9, twin_src, twin_dst, me_s, (1 - me_hi) * columns + me_x)
        ubar1 = net.pull_back(1, [rounded(gain * window[i]) for i in (0, 1)])
        for i in (0, 1):
            ubar_ref[i] = ubar1[i]
        arrived(4, d_dst)
        total = summed(d_dst)
        open_window(3, [total[0], total[1]], 1, edge2_src, edge2_dst)

    arrived(5, m_dst)
    e_src[...] = jnp.stack(row.normal(slots_of(m_dst)), axis=1).astype(BF)
    share = parts // columns
    near(7, e_src.at[pl.ds(me_x * share, share)], share_dst.at[me_x])

    @pl.loop(1, columns)
    def _(k):
        x = lax.rem(me_x + k, columns)
        far(7, e_src.at[pl.ds(x * share, share)], share_dst.at[me_x], me_s, me_hi * columns + x)

    @pl.when(active)
    def _():
        gain = win[2]
        close_window(3, 2, 1, edge2_dst)
        w0 = weight_ref[0]
        w1 = weight_ref[1]
        mbar0 = [
            rounded(gain * window[i] - w1 * win[3 + i] + gain * ubar_ref[i]) for i in (0, 1)
        ]
        ubar0 = net.pull_back(0, mbar0)
        kept = w0 + (1.0 - w0)
        out = [
            (w1 + kept * (1.0 - w1)) * window[i] + kept * ubar_ref[i] + ubar0[i] for i in (0, 1)
        ]
        t_src[...] = jnp.stack([out[0][inner], out[1][inner]], axis=1).astype(BF)

    arrived(7, share_dst)
    share_src[...] = jnp.sum(share_dst[...].astype(F32), axis=0).astype(BF)
    spot2 = me_hi * block + lax.rem(me_s, block)

    @pl.loop(0, share)
    def _(k):
        j = lax.rem(me_s + k, share)
        p = me_x * share + j
        for hi in (0, 1):
            push(10, share_src.at[j], e_dst.at[spot2], p, hi * columns + my_block)

    pl.when(active)(lambda: to_owners(6, t_src, t_dst))

    def image_block(base_ref):
        halves = e_dst[...].astype(F32)
        total = jnp.swapaxes(halves[:block] + halves[block:], 0, 1)
        for i in (0, 1):
            image_src[0, i] = (base_ref[i] - weight_ref[1] * total[i]).astype(BF)

    arrived(10, e_dst)
    pl.when(jnp.logical_not(active))(lambda: arrived(9, twin_dst))
    whenever(active, lambda: image_block(twin_src), lambda: image_block(twin_dst))

    @pl.loop(0, columns)
    def _(x):
        push(8, image_src.at[0], image_dst.at[me_x], me_s, me_hi * columns + x)

    arrived(6, t_dst)
    real, imag = row.expand(slots_of(t_dst))
    grad_ref[:, 0, :] = packed([row.mask * real, row.mask * imag], half)
    arrived(8, image_dst)
    for x in range(columns):
        image_ref[x * block : x * block + block] = packed([image_dst[x, i].astype(F32) for i in (0, 1)], half)

    left(0, maps_ref.at[pl.ds(0, parts - 1)])
    left(2, cot_ref.at[pl.ds(0, parts - 1)])
    if columns > 1:
        whenever(active, lambda: left(1, gain_ref.at[pl.ds(0, columns - 1)]), lambda: left(1, gain_ref))
    else:
        pl.when(jnp.logical_not(active))(lambda: left(1, gain_ref))
    for index, src in ((3, y_src), (4, d_src)):
        whenever(
            to_self,
            functools.partial(left, index, src.at[pl.ds(0, parts - 1)]),
            functools.partial(left, index, src),
        )

    if columns > 1:
        left(7, share_dst.at[pl.ds(0, columns - 1)])
    whenever(
        jnp.logical_and(me_x == my_block, me_x == lax.div(me_s, share)),
        functools.partial(left, 10, e_dst.at[pl.ds(0, 2 * share - 1)]),
        functools.partial(left, 10, e_dst),
    )
    if columns > 1:
        left(8, image_src)

    @pl.when(active)
    def _():
        for index, like in ((5, y_dst), (6, y_dst)):
            whenever(
                to_self,
                functools.partial(left, index, like.at[pl.ds(0, block * coil_parts - 1)]),
                functools.partial(left, index, like),
            )
        left(9, twin_src)
        for which, src in ((0, edge_src), (1, edge2_src)):
            for side, there in ((0, me_x > 0), (1, me_x < columns - 1)):
                def gone(which=which, side=side, src=src):
                    pltpu.make_async_copy(
                        src.at[side], src.at[side], edge_send.at[which * 2 + side]
                    ).wait()

                pl.when(there)(gone)


VMEM = pl.BlockSpec(memory_space=pltpu.VMEM)
SMEM = pl.BlockSpec(memory_space=pltpu.SMEM)


def body(kspace, coil_maps, sampling, dc_weight, kernel_in, bias_in, kernel_out, bias_out, cotangent):
    coils, slots, _, width_two = kspace.shape
    rows = coil_maps.shape[2]
    half = width_two // 2
    volumes, depth, _ = sampling.shape
    coil_parts = lax.axis_size("coil")
    parts = lax.axis_size("section")
    columns = coil_parts // 2
    block = rows // columns
    high = block + 2 * HALO

    cosine, sine = line_tables(half)
    zcos, zsin = depth_tables(depth, volumes * coils)
    operands = (
        coil_maps[:, 0], cotangent[0], sampling.reshape(slots, half), kspace.reshape(coils * slots, width_two),
        cosine, sine, zcos, zsin,
    )

    pair = pltpu.VMEM((slots, 2, WIDE), BF)
    gathered = pltpu.VMEM((coil_parts * block, 2, WIDE), BF)
    owned = pltpu.VMEM((block, 2, WIDE), BF)
    plane2 = pltpu.VMEM((2, high, WIDE), F32)
    hidden = pltpu.VMEM((HID, high, WIDE), F32)
    image, grad = pl.pallas_call(
        functools.partial(cascade_kernel, parts, coil_parts),
        out_shape=(
            jax.ShapeDtypeStruct((rows, width_two), F32),
            jax.ShapeDtypeStruct((coils * slots, 1, width_two), F32),
        ),
        in_specs=[SMEM] * 5 + [pl.BlockSpec(memory_space=pl.ANY)] * 8,
        out_specs=(VMEM, VMEM),
        scratch_shapes=[
            *(pltpu.VMEM(x.shape, x.dtype) for x in operands),
            pltpu.SemaphoreType.DMA((8,)),
            pltpu.VMEM((rows, coils, width_two), BF),
            pltpu.VMEM((rows, 2, WIDE), BF),
            pltpu.VMEM((columns, block, WIDE), BF),
            pltpu.VMEM((2, rows + 2 * HALO, WIDE), F32),
            pltpu.VMEM((slots, coils, width_two), BF),
            pair,
            pltpu.VMEM((coil_parts, block, WIDE), BF),
            pair, gathered, pair, gathered, pair,
            pltpu.VMEM((columns, parts // columns, 2, WIDE), BF),
            pltpu.VMEM((parts // columns, 2, WIDE), BF),
            pltpu.VMEM((2 * block, 2, WIDE), BF),
            pltpu.VMEM((2, 3, HALO, WIDE), BF), pltpu.VMEM((2, 3, HALO, WIDE), BF),
            pltpu.VMEM((2, 2, HALO, WIDE), BF), pltpu.VMEM((2, 2, HALO, WIDE), BF),
            pltpu.VMEM((5, high, WIDE), F32),
            owned, pair, owned, pair,
            pltpu.VMEM((max(columns - 1, 1), 2, block, WIDE), BF),
            pltpu.VMEM((columns, 2, block, WIDE), BF),
            pltpu.VMEM((2, block, WIDE), F32), pltpu.VMEM((2, block, WIDE), F32),
            plane2, plane2,
            hidden, hidden, pltpu.VMEM((2, HID, high, WIDE), F32),
            pltpu.SemaphoreType.DMA((11,)), pltpu.SemaphoreType.DMA((11,)),
            pltpu.SemaphoreType.DMA((4,)), pltpu.SemaphoreType.DMA((4,)),
        ],
        compiler_params=pltpu.CompilerParams(collective_id=0, has_side_effects=True),
        name="cascade",
    )(
        jnp.swapaxes(kernel_in, 2, 3), bias_in, kernel_out, bias_out, dc_weight, *operands,
    )
    return image[None], grad.reshape(coils, slots, 1, width_two)


def solution(mesh):
    return jax.shard_map(
        body,
        mesh=mesh,
        in_specs=(
            P("coil", None, "section", None),
            P("coil", "section", None, None),
            P(), P(), P(), P(), P(), P(),
            P("section", None, None),
        ),
        out_specs=(P("section", None, None), P("coil", None, "section", None)),
        check_vma=False,
    )
```

```python
import functools
import math

import jax
import jax.numpy as jnp
import numpy as np
from jax import lax
from jax.experimental import pallas as pl
from jax.experimental.pallas import tpu as pltpu
from jax.sharding import PartitionSpec as P

BF = jnp.bfloat16
F32 = jnp.float32
HID = 18
WIDE = 384
HALO = 8


def tables(count, wide):
    index = np.arange(count)
    angle = (index[:, None] * index[None, :] % count) * (2.0 * math.pi / count)
    cosine = np.zeros((wide, wide), np.float32)
    sine = np.zeros((wide, wide), np.float32)
    cosine[:count, :count] = np.cos(angle) / math.sqrt(count)
    sine[:count, :count] = np.sin(angle) / math.sqrt(count)
    return cosine, sine


def line_tables(count):
    cosine, sine = tables(count, WIDE)
    return jnp.asarray(cosine).astype(BF), jnp.asarray(sine).astype(BF)


def depth_tables(depth, blocks):
    cosine, sine = tables(depth, depth)
    eye = np.eye(blocks, dtype=np.float32)
    return jnp.asarray(np.kron(eye, cosine)).astype(BF), jnp.asarray(np.kron(eye, sine)).astype(BF)


def dot(a, b):
    return jnp.dot(a, b, preferred_element_type=F32)


def line_transform(real, imag, cosine, sine, sign):
    rows = real.shape[0]
    both = jnp.concatenate([real, imag], axis=0).astype(BF)
    straight = dot(both, cosine)
    crossed = dot(both, sine)
    return straight[:rows] - sign * crossed[rows:], straight[rows:] + sign * crossed[:rows]


def depth_transform(real, imag, cosine, sine, sign):
    both = jnp.concatenate([real, imag], axis=1).astype(BF)
    straight = dot(cosine, both)
    crossed = dot(sine, both)
    return (
        straight[:, :WIDE] - sign * crossed[:, WIDE:],
        straight[:, WIDE:] + sign * crossed[:, :WIDE],
    )


class Row:
    def __init__(self, mask, line, depth):
        self.mask = mask
        self.line = line
        self.depth = depth

    def take_maps(self, planes):
        self.coils = planes.shape[0]
        stacked = jnp.concatenate([planes[i] for i in range(self.coils)], axis=0)
        self.maps_real, self.maps_imag = planes_of(stacked)

    def expand(self, picture):
        real = jnp.concatenate([picture[0]] * self.coils, axis=0)
        imag = jnp.concatenate([picture[1]] * self.coils, axis=0)
        out = (
            self.maps_real * real - self.maps_imag * imag,
            self.maps_real * imag + self.maps_imag * real,
        )
        out = line_transform(*out, *self.line, -1.0)
        return depth_transform(*out, *self.depth, -1.0)

    def inverse(self, real, imag):
        real, imag = depth_transform(real, imag, *self.depth, 1.0)
        return line_transform(real, imag, *self.line, 1.0)

    def collect(self, real, imag):
        out_real = self.maps_real * real + self.maps_imag * imag
        out_imag = self.maps_real * imag - self.maps_imag * real
        n = out_real.shape[0] // self.coils
        return [
            sum(out[i * n : i * n + n] for i in range(self.coils)) for out in (out_real, out_imag)
        ]

    def normal(self, picture):
        real, imag = self.expand(picture)
        return self.collect(*self.inverse(self.mask * real, self.mask * imag))


def shifted(x, down, right):
    if down:
        x = pltpu.roll(x, (-down) % x.shape[0], 0)
    if right:
        x = pltpu.roll(x, (-right) % x.shape[1], 1)
    return x


def widen(x):
    return jnp.concatenate([x, jnp.zeros((x.shape[0], WIDE - x.shape[1]), x.dtype)], axis=1)


def planes_of(x):
    half = x.shape[1] // 2
    return [widen(x[:, :half].astype(F32)), widen(x[:, half:].astype(F32))]


def packed(planes, half):
    return jnp.concatenate([planes[0][:, :half], planes[1][:, :half]], axis=1)


def rounded(x):
    return x.astype(BF).astype(F32)


class Refiner:
    def __init__(self, kin_ref, bin_ref, kout_ref, bout_ref, inside, taps_ref, hidden_ref, slope_ref):
        self.kin, self.bin, self.kout, self.bout = kin_ref, bin_ref, kout_ref, bout_ref
        self.inside = inside
        self.taps, self.hidden, self.slope = taps_ref, hidden_ref, slope_ref

    def spread_taps(self, planes, sign):
        for channel in (0, 1):
            for b in range(3):
                moved = shifted(planes[channel], 0, sign * (b - 1))
                for a in range(3):
                    self.taps[(a * 3 + b) * 2 + channel] = shifted(moved, sign * (a - 1), 0)

    def gather_taps(self, sign):
        planes = []
        for channel in (0, 1):
            plane = None
            for b in range(3):
                column = None
                for a in range(3):
                    piece = shifted(self.taps[(a * 3 + b) * 2 + channel], sign * (a - 1), 0)
                    column = piece if column is None else column + piece
                column = shifted(column, 0, sign * (b - 1))
                plane = column if plane is None else plane + column
            planes.append(plane)
        return planes

    @staticmethod
    def mix(source_ref, weight_of, first):
        total = first
        for k in range(HID):
            term = weight_of(k) * source_ref[k]
            total = term if total is None else total + term
        return total

    def into_hidden(self, t, o, k):
        return self.kin[t, k // 2, k % 2, o]

    def out_of_hidden(self, t, k, o):
        if isinstance(k, int):
            return self.kout[t, k // 2, k % 2, o]
        return self.kout[t, lax.div(k, 2), lax.rem(k, 2), o]

    def refine(self, t, planes):
        self.spread_taps(planes, 1)

        @pl.loop(0, HID)
        def _(o):
            first = jnp.full(self.inside.shape, self.bin[t, o], F32)
            pre = self.mix(self.taps, lambda k: self.into_hidden(t, o, k), first)
            gate = jax.nn.sigmoid(pre)
            self.hidden[o] = self.inside * pre * gate
            self.slope[t, o] = self.inside * gate * (1.0 + pre * (1.0 - gate))

        @pl.loop(0, HID)
        def _(k):
            self.taps[k] = self.mix(self.hidden, lambda o: self.out_of_hidden(t, k, o), None)

        planes = self.gather_taps(1)
        return [rounded(planes[i] + self.bout[t, i]) for i in (0, 1)]

    def pull_back(self, t, planes):
        self.spread_taps(planes, -1)

        @pl.loop(0, HID)
        def _(o):
            self.hidden[o] = self.slope[t, o] * self.mix(
                self.taps, lambda k: self.out_of_hidden(t, k, o), None
            )

        @pl.loop(0, HID)
        def _(k):
            tap = lax.div(k, 2)
            channel = lax.rem(k, 2)
            self.taps[k] = self.mix(self.hidden, lambda o: self.kin[t, tap, channel, o], None)

        return [rounded(x) for x in self.gather_taps(-1)]


def in_groups(first, last, act):
    count = last - first
    group = next(n for n in (9, 8, 7, 5, 3, 1) if count % n == 0)

    @pl.loop(0, count // group)
    def _(g):
        for k in range(group):
            act(first + g * group + k)


def clear(first_ref, second_ref, side):
    first_ref[side] = jnp.zeros(first_ref.shape[1:], first_ref.dtype)
    second_ref[side] = jnp.zeros(second_ref.shape[1:], second_ref.dtype)


def cascade_kernel(
    parts, coil_parts,
    kin_ref, bin_ref, kout_ref, bout_ref, weight_ref,
    maps_any, cot_any, sampling_any, k_any, c_any, s_any, zc_any, zs_any,
    image_ref, grad_ref,
    maps_in, cot_in, sampling_in, k_ref, c_ref, s_ref, zc_ref, zs_ref, load,
    maps_ref, cot_ref, gain_ref, cot_pad,
    maps_row, cot_row, gain_all,
    y_src, y_dst, d_src, d_dst, e_src, share_dst, share_src, e_dst,
    edge_src, edge_dst, edge2_src, edge2_dst, win,
    m_src, m_dst, t_src, t_dst, image_src, image_dst, twin_src, twin_dst, state_ref, ubar_ref,
    taps_ref, hidden_ref, slope_ref,
    send, recv, edge_send, edge_recv,
):
    rows = maps_ref.shape[0]
    half = sampling_in.shape[1]
    columns = coil_parts // 2
    block = rows // columns
    me_s = lax.axis_index("section")
    me_c = lax.axis_index("coil")
    me_x = lax.rem(me_c, columns)
    me_hi = lax.div(me_c, columns)
    my_block = lax.div(me_s, block)
    active = me_hi == lax.rem(me_s, 2)
    to_self = jnp.logical_and(active, me_x == my_block)

    def holder(slot, x):
        return lax.rem(slot, 2) * columns + x

    def whenever(condition, yes, no=None):
        pl.when(condition)(yes)
        if no is not None:
            pl.when(jnp.logical_not(condition))(no)

    def near(index, src, dst):
        pltpu.make_async_copy(src, dst, recv.at[index]).start()

    def far(index, src, dst, section, coil):
        pltpu.make_async_remote_copy(
            src, dst, send.at[index], recv.at[index],
            device_id={"section": section, "coil": coil}, device_id_type=pl.DeviceIdType.MESH,
        ).start()

    def push(index, src, dst, section, coil):
        mine = jnp.logical_and(section == me_s, coil == me_c)
        whenever(
            mine,
            lambda: near(index, src, dst),
            lambda: far(index, src, dst, section, coil),
        )

    def arrived(index, ref):
        pltpu.make_async_copy(ref, ref, recv.at[index]).wait()

    def left(index, ref):
        pltpu.make_async_copy(ref, ref, send.at[index]).wait()

    barrier = pltpu.get_barrier_semaphore()

    def greet(section, coil):
        pl.semaphore_signal(
            barrier, 1, device_id={"section": section, "coil": coil}, device_id_type=pl.DeviceIdType.MESH
        )

    in_groups(1, parts, lambda k: greet(lax.rem(me_s + k, parts), me_c))
    in_groups(1, coil_parts, lambda k: greet(me_s, lax.rem(me_c + k, coil_parts)))

    loads = [
        pltpu.make_async_copy(src, dst, load.at[i])
        for i, (src, dst) in enumerate(
            zip(
                (maps_any, cot_any, sampling_any, k_any, c_any, s_any, zc_any, zs_any),
                (maps_in, cot_in, sampling_in, k_ref, c_ref, s_ref, zc_ref, zs_ref),
            )
        )
    ]
    for copy in loads:
        copy.start()

    loads[0].wait()
    maps_ref[...] = jnp.swapaxes(maps_in[...], 0, 1)
    gain = None
    for i in range(maps_in.shape[0]):
        for plane in planes_of(maps_in[i]):
            gain = plane * plane if gain is None else gain + plane * plane
    for x in range(columns):
        gain_ref[x] = gain[x * block : x * block + block].astype(BF)
    loads[1].wait()
    cot_planes = planes_of(cot_in[...])
    cot_ref[...] = jnp.stack(cot_planes, axis=1).astype(BF)
    for i in (0, 1):
        cot_pad[i, :HALO] = jnp.zeros((HALO, WIDE), F32)
        cot_pad[i, HALO + rows :] = jnp.zeros((HALO, WIDE), F32)
        cot_pad[i, HALO : HALO + rows] = cot_planes[i]
    high = block + 2 * HALO
    first_row = pl.multiple_of(me_x * block, HALO)
    window = [cot_pad[i, pl.ds(first_row, high), :] for i in (0, 1)]
    place = first_row - HALO + lax.broadcasted_iota(jnp.int32, (high, WIDE), 0)
    line = lax.broadcasted_iota(jnp.int32, (high, WIDE), 1)
    inside = jnp.where((place >= 0) & (place < rows) & (line < half), 1.0, 0.0).astype(F32)
    loads[2].wait()
    mask = widen(sampling_in[...].astype(F32))

    pl.semaphore_wait(barrier, parts - 1 + coil_parts - 1)

    def to_section(index, src, dst):
        near(index, src.at[me_s], dst.at[me_s])

        def send_to(k):
            p = lax.rem(me_s + k, parts)
            far(index, src.at[p], dst.at[me_s], p, me_c)

        in_groups(1, parts, send_to)

    to_section(0, maps_ref, maps_row)

    @pl.loop(0, columns)
    def _(x):
        push(1, gain_ref.at[x], gain_all.at[me_c], me_s, holder(me_s, x))

    @pl.loop(0, block)
    def _(k):
        r = me_x * block + lax.rem(me_s + k, block)
        push(2, cot_ref.at[r], cot_row.at[me_s], r, me_c)

    pl.when(me_x == 0)(lambda: clear(edge_dst, edge2_dst, 0))
    pl.when(me_x == columns - 1)(lambda: clear(edge_dst, edge2_dst, 1))

    spot = me_c * block + lax.rem(me_s, block)

    def to_holders(index, src, dst):
        push(index, src.at[me_s], dst.at[spot], me_s, holder(me_s, my_block))

        def send_to(k):
            p = lax.rem(me_s + k, parts)
            far(index, src.at[p], dst.at[spot], p, holder(p, my_block))

        in_groups(1, parts, send_to)

    def to_owners(index, src, dst):
        @pl.loop(0, block)
        def _(i):
            push(index, src.at[i], dst.at[me_s], me_x * block + i, me_c)

            for k in range(1, coil_parts):
                far(index, src.at[i], dst.at[me_s], me_x * block + i, lax.rem(me_c + k, coil_parts))

    def slots_of(ref):
        return jnp.swapaxes(ref[...].astype(F32), 0, 1)

    def summed(ref):
        all_parts = ref[...].astype(F32)
        total = all_parts[:block]
        for q in range(1, coil_parts):
            total = total + all_parts[q * block : q * block + block]
        return jnp.swapaxes(total, 0, 1)

    coils = maps_in.shape[0]
    for copy in loads[3:]:
        copy.wait()
    row = Row(
        jnp.concatenate([mask] * coils, axis=0),
        (c_ref[...], s_ref[...]), (zc_ref[...], zs_ref[...]),
    )
    weighted = weight_ref[0] * row.mask
    start = []
    for part in planes_of(k_ref[...]):
        measured = row.mask * part
        start.append(measured - weighted * (measured - measured))
    images = row.inverse(*start)
    arrived(0, maps_row)
    row.take_maps(slots_of(maps_row))
    y_src[...] = jnp.stack(row.collect(*images), axis=1).astype(BF)
    to_holders(3, y_src, y_dst)
    arrived(2, cot_row)

    def relays():
        return [
            pltpu.make_async_remote_copy(
                cot_row, cot_row, send.at[10 + k], recv.at[2],
                device_id={"section": me_s, "coil": me_hi * columns + lax.rem(me_x + k, columns)},
                device_id_type=pl.DeviceIdType.MESH,
            )
            for k in range(1, columns)
        ]

    pl.when(me_x == my_block)(lambda: [copy.start() for copy in relays()] and None)
    d_src[...] = jnp.stack(row.normal(slots_of(cot_row)), axis=1).astype(BF)
    to_holders(4, d_src, d_dst)

    def exchange_edges(which, src, dst):
        def link(side, coil):
            return pltpu.make_async_remote_copy(
                src.at[side], dst.at[1 - side],
                edge_send.at[which * 2 + side], edge_recv.at[which * 2 + 1 - side],
                device_id={"section": me_s, "coil": coil}, device_id_type=pl.DeviceIdType.MESH,
            )

        pl.when(me_x > 0)(lambda: link(0, me_c - 1).start())
        pl.when(me_x < columns - 1)(lambda: link(1, me_c + 1).start())

    def open_window(first, planes, which, src, dst):
        for i, plane in enumerate(planes):
            plane = rounded(plane)
            win[first + i, HALO : HALO + block] = plane
            src[0, i] = plane[:HALO].astype(BF)
            src[1, i] = plane[block - HALO :].astype(BF)
        exchange_edges(which, src, dst)

    def close_window(first, count, which, dst):
        def coming(side):
            pltpu.make_async_copy(dst.at[side], dst.at[side], edge_recv.at[which * 2 + side]).wait()

        pl.when(me_x > 0)(lambda: coming(0))
        pl.when(me_x < columns - 1)(lambda: coming(1))
        for i in range(count):
            win[first + i, :HALO] = dst[0, i].astype(F32)
            win[first + i, HALO + block :] = dst[1, i].astype(F32)

    inner = slice(HALO, HALO + block)

    net = Refiner(kin_ref, bin_ref, kout_ref, bout_ref, inside, taps_ref, hidden_ref, slope_ref)

    @pl.when(active)
    def _():
        arrived(1, gain_all)
        gains = jnp.sum(gain_all[...].astype(F32), axis=0)
        arrived(3, y_dst)
        total = summed(y_dst)
        open_window(0, [total[0], total[1], gains], 0, edge_src, edge_dst)
        close_window(0, 3, 0, edge_dst)
        m0 = net.refine(0, [rounded(win[0]), rounded(win[1])])
        m_src[...] = jnp.stack([m0[0][inner], m0[1][inner]], axis=1).astype(BF)
        to_owners(5, m_src, m_dst)
        for i in (0, 1):
            state_ref[i] = win[i] + win[2] * m0[i]
        gain = win[2]
        m1 = net.refine(1, [rounded(state_ref[0]), rounded(state_ref[1])])
        for i in (0, 1):
            twin_src[i] = (state_ref[i] + gain * m1[i])[inner]
        far(9, twin_src, twin_dst, me_s, (1 - me_hi) * columns + me_x)
        ubar1 = net.pull_back(1, [rounded(gain * window[i]) for i in (0, 1)])
        for i in (0, 1):
            ubar_ref[i] = ubar1[i]
        arrived(4, d_dst)
        total = summed(d_dst)
        open_window(3, [total[0], total[1]], 1, edge2_src, edge2_dst)

    arrived(5, m_dst)
    e_src[...] = jnp.stack(row.normal(slots_of(m_dst)), axis=1).astype(BF)
    share = parts // columns
    near(7, e_src.at[pl.ds(me_x * share, share)], share_dst.at[me_x])

    @pl.loop(1, columns)
    def _(k):
        x = lax.rem(me_x + k, columns)
        far(7, e_src.at[pl.ds(x * share, share)], share_dst.at[me_x], me_s, me_hi * columns + x)

    @pl.when(active)
    def _():
        gain = win[2]
        close_window(3, 2, 1, edge2_dst)
        w0 = weight_ref[0]
        w1 = weight_ref[1]
        mbar0 = [
            rounded(gain * window[i] - w1 * win[3 + i] + gain * ubar_ref[i]) for i in (0, 1)
        ]
        ubar0 = net.pull_back(0, mbar0)
        kept = w0 + (1.0 - w0)
        out = [
            (w1 + kept * (1.0 - w1)) * window[i] + kept * ubar_ref[i] + ubar0[i] for i in (0, 1)
        ]
        t_src[...] = jnp.stack([out[0][inner], out[1][inner]], axis=1).astype(BF)

    arrived(7, share_dst)
    share_src[...] = jnp.sum(share_dst[...].astype(F32), axis=0).astype(BF)
    spot2 = me_hi * block + lax.rem(me_s, block)

    @pl.loop(0, share)
    def _(k):
        j = lax.rem(me_s + k, share)
        p = me_x * share + j
        for hi in (0, 1):
            push(10, share_src.at[j], e_dst.at[spot2], p, hi * columns + my_block)

    pl.when(active)(lambda: to_owners(6, t_src, t_dst))

    def image_block(base_ref):
        halves = e_dst[...].astype(F32)
        total = jnp.swapaxes(halves[:block] + halves[block:], 0, 1)
        for i in (0, 1):
            image_src[0, i] = (base_ref[i] - weight_ref[1] * total[i]).astype(BF)

    arrived(10, e_dst)
    pl.when(jnp.logical_not(active))(lambda: arrived(9, twin_dst))
    whenever(active, lambda: image_block(twin_src), lambda: image_block(twin_dst))

    @pl.loop(0, columns)
    def _(x):
        push(8, image_src.at[0], image_dst.at[me_x], me_s, me_hi * columns + x)

    arrived(6, t_dst)
    real, imag = row.expand(slots_of(t_dst))
    grad_ref[:, 0, :] = packed([row.mask * real, row.mask * imag], half)
    arrived(8, image_dst)
    for x in range(columns):
        image_ref[x * block : x * block + block] = packed([image_dst[x, i].astype(F32) for i in (0, 1)], half)

    left(0, maps_ref.at[pl.ds(0, parts - 1)])
    whenever(
        me_x == my_block,
        functools.partial(left, 2, cot_ref.at[pl.ds(0, block - 1)]),
        functools.partial(left, 2, cot_ref.at[pl.ds(0, block)]),
    )
    for k in range(1, columns):
        pl.when(me_x == my_block)(functools.partial(left, 10 + k, cot_row))
    if columns > 1:
        whenever(active, lambda: left(1, gain_ref.at[pl.ds(0, columns - 1)]), lambda: left(1, gain_ref))
    else:
        pl.when(jnp.logical_not(active))(lambda: left(1, gain_ref))
    for index, src in ((3, y_src), (4, d_src)):
        whenever(
            to_self,
            functools.partial(left, index, src.at[pl.ds(0, parts - 1)]),
            functools.partial(left, index, src),
        )

    if columns > 1:
        left(7, share_dst.at[pl.ds(0, columns - 1)])
    whenever(
        jnp.logical_and(me_x == my_block, me_x == lax.div(me_s, share)),
        functools.partial(left, 10, e_dst.at[pl.ds(0, 2 * share - 1)]),
        functools.partial(left, 10, e_dst),
    )
    if columns > 1:
        left(8, image_src)

    @pl.when(active)
    def _():
        for index, like in ((5, y_dst), (6, y_dst)):
            whenever(
                to_self,
                functools.partial(left, index, like.at[pl.ds(0, block * coil_parts - 1)]),
                functools.partial(left, index, like),
            )
        left(9, twin_src)
        for which, src in ((0, edge_src), (1, edge2_src)):
            for side, there in ((0, me_x > 0), (1, me_x < columns - 1)):
                def gone(which=which, side=side, src=src):
                    pltpu.make_async_copy(
                        src.at[side], src.at[side], edge_send.at[which * 2 + side]
                    ).wait()

                pl.when(there)(gone)


VMEM = pl.BlockSpec(memory_space=pltpu.VMEM)
SMEM = pl.BlockSpec(memory_space=pltpu.SMEM)


def body(kspace, coil_maps, sampling, dc_weight, kernel_in, bias_in, kernel_out, bias_out, cotangent):
    coils, slots, _, width_two = kspace.shape
    rows = coil_maps.shape[2]
    half = width_two // 2
    volumes, depth, _ = sampling.shape
    coil_parts = lax.axis_size("coil")
    parts = lax.axis_size("section")
    columns = coil_parts // 2
    block = rows // columns
    high = block + 2 * HALO

    cosine, sine = line_tables(half)
    zcos, zsin = depth_tables(depth, volumes * coils)
    operands = (
        coil_maps[:, 0], cotangent[0], sampling.reshape(slots, half), kspace.reshape(coils * slots, width_two),
        cosine, sine, zcos, zsin,
    )

    pair = pltpu.VMEM((slots, 2, WIDE), BF)
    gathered = pltpu.VMEM((coil_parts * block, 2, WIDE), BF)
    owned = pltpu.VMEM((block, 2, WIDE), BF)
    plane2 = pltpu.VMEM((2, high, WIDE), F32)
    hidden = pltpu.VMEM((HID, high, WIDE), F32)
    image, grad = pl.pallas_call(
        functools.partial(cascade_kernel, parts, coil_parts),
        out_shape=(
            jax.ShapeDtypeStruct((rows, width_two), F32),
            jax.ShapeDtypeStruct((coils * slots, 1, width_two), F32),
        ),
        in_specs=[SMEM] * 5 + [pl.BlockSpec(memory_space=pl.ANY)] * 8,
        out_specs=(VMEM, VMEM),
        scratch_shapes=[
            *(pltpu.VMEM(x.shape, x.dtype) for x in operands),
            pltpu.SemaphoreType.DMA((8,)),
            pltpu.VMEM((rows, coils, width_two), BF),
            pltpu.VMEM((rows, 2, WIDE), BF),
            pltpu.VMEM((columns, block, WIDE), BF),
            pltpu.VMEM((2, rows + 2 * HALO, WIDE), F32),
            pltpu.VMEM((slots, coils, width_two), BF),
            pair,
            pltpu.VMEM((coil_parts, block, WIDE), BF),
            pair, gathered, pair, gathered, pair,
            pltpu.VMEM((columns, parts // columns, 2, WIDE), BF),
            pltpu.VMEM((parts // columns, 2, WIDE), BF),
            pltpu.VMEM((2 * block, 2, WIDE), BF),
            pltpu.VMEM((2, 3, HALO, WIDE), BF), pltpu.VMEM((2, 3, HALO, WIDE), BF),
            pltpu.VMEM((2, 2, HALO, WIDE), BF), pltpu.VMEM((2, 2, HALO, WIDE), BF),
            pltpu.VMEM((5, high, WIDE), F32),
            owned, pair, owned, pair,
            pltpu.VMEM((max(columns - 1, 1), 2, block, WIDE), BF),
            pltpu.VMEM((columns, 2, block, WIDE), BF),
            pltpu.VMEM((2, block, WIDE), F32), pltpu.VMEM((2, block, WIDE), F32),
            plane2, plane2,
            hidden, hidden, pltpu.VMEM((2, HID, high, WIDE), F32),
            pltpu.SemaphoreType.DMA((10 + columns,)), pltpu.SemaphoreType.DMA((11,)),
            pltpu.SemaphoreType.DMA((4,)), pltpu.SemaphoreType.DMA((4,)),
        ],
        compiler_params=pltpu.CompilerParams(collective_id=0, has_side_effects=True),
        name="cascade",
    )(
        jnp.swapaxes(kernel_in, 2, 3), bias_in, kernel_out, bias_out, dc_weight, *operands,
    )
    return image[None], grad.reshape(coils, slots, 1, width_two)


def solution(mesh):
    return jax.shard_map(
        body,
        mesh=mesh,
        in_specs=(
            P("coil", None, "section", None),
            P("coil", "section", None, None),
            P(), P(), P(), P(), P(), P(),
            P("section", None, None),
        ),
        out_specs=(P("section", None, None), P("coil", None, "section", None)),
        check_vma=False,
    )
```
